32 devices in a mesh: groups: 2 (over x), kv: 16 (over z, y, core).
Axes of the slice: x: 2, y: 2, z: 4, core: 2. Of those that a mesh axis runs over, the one named last changes fastest.
Arguments:
- query_in: bfloat16 [256, 2048], P(('groups', 'kv')), parts along dimension 0, may hold values from -6 to 6
- key_in: bfloat16 [256, 512], P(('groups', 'kv')), parts along dimension 0, may hold values from -16 to 16
- value_in: bfloat16 [256, 512], P(('groups', 'kv')), parts along dimension 0, may hold values from -6 to 6
- cache_keys: bfloat16 [4, 6144, 512], P('groups', 'kv'), parts along dimension 0, may hold values from -700 to 700
- cache_values: bfloat16 [4, 6144, 512], P('groups', 'kv'), parts along dimension 0, may hold values from -6 to 6
- live_slots: int32 [4, 16], P('groups', 'kv'), parts along dimension 0, may hold values from 0 to 384, as said below
- span_starts: int32 [4], P('groups'), parts along dimension 0, may hold values from 0 to 1048447
Outputs:
- attended: bfloat16 [256, 2048], P(('groups', 'kv')), parts along dimension 0
The draws below stay inside these ranges and needn't reach their ends.
There are 2 independent parts, one for each index of `groups`. The reference program is written for one: setup_inputs(seed, part) draws one part's arguments, and reference() takes and returns one part's arrays. A program takes and returns all parts, laid end to end along the dimension named above; each array names one. Nothing has to cross between parts.
Inputs may be any that keep to these rules, and one draw needn't show every extreme that they name: `live_slots`: in every block some device has all 384 of its slots live.
All inputs are finite; a program needn't handle non-finite values.
Results may differ from the reference program's by a relative error of at most 0.006.
The reference program's roundings to bfloat16 on the way count: a program that leaves them out, or rounds other values in their place, can miss the bound.
Values may be sent and summed in bfloat16 or wider, within the bound.
No kernel may reach another device: no remote copies, remote signals or barrier semaphores. Data moves between devices by JAX's collectives and lax.ppermute only.
A program may use at most 320 MiB of HBM per device.

```python
import jax
import jax.numpy as jnp
import numpy as np
from jax import lax

H = 16
KVH = 4
HD = 128
CH = 64
SPANS = 2
SLOT_DEV = 384
TOK = 128
SLOTS = 6144
N_KV = 16


def draw_cache_keys(key, part):
    base_draw = 3.5 * jax.random.normal(jax.random.fold_in(key, 11), (SPANS, SLOTS, KVH * HD), jnp.float32)
    return jnp.clip(base_draw, -700.0, 700.0).astype(jnp.bfloat16)


def draw_live_slots(key, part):
    shard_count = SLOTS // SLOT_DEV
    live_counts = jax.random.randint(jax.random.fold_in(key, 21), (SPANS, shard_count), 0, SLOT_DEV + 1)
    full_shard = jax.random.randint(jax.random.fold_in(key, 22), (SPANS,), 0, shard_count)
    filled = jnp.arange(shard_count)[None, :] == full_shard[:, None]
    return jnp.where(filled, SLOT_DEV, live_counts).astype(jnp.int32)


def block_levels(key, dims, cuts, low, top_value):
    level, own = 1.0, jax.random.fold_in(key, 6)
    for dim, parts in cuts:
        heights = jnp.exp(jax.random.uniform(jax.random.fold_in(own, dim), (parts,), jnp.float32, low / len(cuts), top_value / len(cuts)))
        level = level * jnp.repeat(heights, dims[dim] // parts).reshape([-1 if axis == dim else 1 for axis in range(len(dims))])
    return level


def gaussian(rng, dims, spread, limit, split=(), held_as=jnp.bfloat16):
    array = jax.random.normal(rng, dims, jnp.float32) * spread
    if len(split) > 0:
        array = block_levels(rng, dims, split, -0.22, 0.18) * array
    return jnp.clip(array, min=-limit, max=limit).astype(held_as)


def setup_inputs(seed: int = 0, part: int = 0) -> dict:
    splits = jax.random.split(jax.random.key(seed), 8)
    part_keys = jax.random.split(jax.random.fold_in(splits[7], part), 8)
    query_in = gaussian(part_keys[0], (TOK, H * HD), 1.0, 6.0, ((0, 16),))
    key_in = gaussian(part_keys[1], (TOK, KVH * HD), 3.5, 16.0, ((0, 16),))
    value_in = gaussian(part_keys[2], (TOK, KVH * HD), 1.0, 6.0, ((0, 16),))
    cache_keys = draw_cache_keys(jax.random.fold_in(jax.random.fold_in(splits[7], part), 71), part)
    cache_values = gaussian(part_keys[4], (SPANS, SLOTS, KVH * HD), 1.0, 6.0, ((1, 16),))
    live_slots = draw_live_slots(jax.random.fold_in(jax.random.fold_in(splits[7], part), 71), part)
    span_starts = jax.random.randint(part_keys[6], (SPANS,), 0, 1048448).astype(jnp.int32)
    return dict(query_in=query_in, key_in=key_in, value_in=value_in, cache_keys=cache_keys, cache_values=cache_values, live_slots=live_slots, span_starts=span_starts)


NEG_FILL = -1e30


def turn_table(head_size):
    half_size = head_size // 2
    frequency = 500000.0 ** (-np.arange(half_size) * 2.0 / head_size)
    turn_counts = np.floor(frequency / (2.0 * np.pi) * 2.0 ** 32 + 0.5).astype(np.int64) % (2 ** 32)
    turn_counts = np.where(turn_counts >= 2 ** 31, turn_counts - 2 ** 32, turn_counts)
    return jnp.asarray(turn_counts.astype(np.int32))


def rotate_pairs(values, positions):
    half_size = values.shape[-1] // 2
    phases = positions[:, None] * turn_table(values.shape[-1])[None, :]
    angles = phases.astype(jnp.float32) * (2.0 * np.pi / 2.0 ** 32)
    cosine = jnp.cos(angles)[:, None, :]
    sine_table = jnp.sin(angles)[:, None, :]
    first_half = values[..., :half_size]
    second_half = values[..., half_size:]
    return jnp.concatenate([first_half * cosine - second_half * sine_table, second_half * cosine + first_half * sine_table], axis=-1)


def settle(values):
    return lax.optimization_barrier(values.astype(jnp.bfloat16)).astype(jnp.float32)


def reference(query_in, key_in, value_in, cache_keys, cache_values, live_slots, span_starts):
    tokens = SPANS * CH
    group_size = H // KVH
    score_scale = HD ** -0.5
    positions = (span_starts[:, None] + jnp.arange(CH, dtype=jnp.int32)[None, :]).reshape(tokens).astype(jnp.int32)
    queries = rotate_pairs(query_in.astype(jnp.float32).reshape(tokens, H, HD), positions).astype(jnp.bfloat16)
    keys_new = rotate_pairs(key_in.astype(jnp.float32).reshape(tokens, KVH, HD), positions).astype(jnp.bfloat16)
    values_new = value_in.reshape(tokens, KVH, HD)
    slot_index = jnp.arange(SLOT_DEV, dtype=jnp.int32)
    results = []
    for span_index in range(SPANS):
        first_row = span_index * CH
        grouped = queries[first_row:first_row + CH].reshape(CH, KVH, group_size, HD).astype(jnp.float32)
        own_keys = keys_new[first_row:first_row + CH].astype(jnp.float32)
        own_values = values_new[first_row:first_row + CH].astype(jnp.float32)
        causal = jnp.arange(CH)[:, None] >= jnp.arange(CH)[None, :]
        own_scores = jnp.einsum('rkgd,skd->kgrs', grouped, own_keys) * score_scale
        own_scores = jnp.where(causal, own_scores, NEG_FILL)
        shard_keys = cache_keys[span_index].reshape(N_KV, SLOT_DEV, KVH, HD)
        shard_values = cache_values[span_index].reshape(N_KV, SLOT_DEV, KVH, HD)
        shard_live = live_slots[span_index]

        def shard_scores(block_keys, live_count):
            scores = jnp.einsum('rkgd,skd->kgrs', grouped, block_keys.astype(jnp.float32)) * score_scale
            allowed = slot_index < live_count
            return jnp.where(allowed, scores, NEG_FILL), allowed

        def shard_max(inputs):
            scores, allowed = shard_scores(inputs[0], inputs[1])
            return jnp.max(scores, axis=-1)

        maxima = lax.map(shard_max, (shard_keys, shard_live))
        row_max = jnp.maximum(jnp.max(maxima, axis=0), jnp.max(own_scores, axis=-1))

        def add_shard(carried, inputs):
            running_total, weighted_sum = carried
            scores, allowed = shard_scores(inputs[0], inputs[2])
            weights = jnp.where(allowed, jnp.exp(scores - row_max[..., None]), 0.0)
            weighted_sum = weighted_sum + jnp.einsum('kgrs,skd->rkgd', settle(weights), inputs[1].astype(jnp.float32))
            return (running_total + jnp.sum(weights, axis=-1), weighted_sum), None

        own_weights = jnp.where(causal, jnp.exp(own_scores - row_max[..., None]), 0.0)
        initial = (jnp.sum(own_weights, axis=-1), jnp.einsum('kgrs,skd->rkgd', settle(own_weights), own_values))
        (running_total, weighted_sum), unused_out = lax.scan(add_shard, initial, (shard_keys, shard_values, shard_live))
        attended = weighted_sum / jnp.transpose(running_total, (2, 0, 1))[..., None]
        results.append(attended.reshape(CH, H * HD))
    return jnp.concatenate(results, axis=0).astype(jnp.bfloat16)
```

```python
import functools

import jax
import jax.numpy as jnp
import numpy as np
from jax import lax
from jax.experimental import pallas as pl
from jax.experimental.pallas import tpu as pltpu
from jax.sharding import PartitionSpec as P

HD = 128
LANES = 128
NEG_FILL = -1e30
MAX_FLOOR = -5e29
BF = jnp.bfloat16
F32 = jnp.float32


def turn_table(head_size):
    half_size = head_size // 2
    frequency = 500000.0 ** (-np.arange(half_size) * 2.0 / head_size)
    turn_counts = np.floor(frequency / (2.0 * np.pi) * 2.0**32 + 0.5).astype(np.int64) % 2**32
    turn_counts = np.where(turn_counts >= 2**31, turn_counts - 2**32, turn_counts)
    return turn_counts.astype(np.int32)


def stages_of(devices):
    core = 2 if devices % 2 == 0 else 1
    rest = devices // core
    inner = 1 << ((rest.bit_length() - 1) // 2)
    outer = rest // inner
    return (core * inner, outer), (core, inner), (1, core)


def swap(values, distance):
    devices = lax.axis_size("kv")
    return lax.ppermute(values, "kv", [(i, i ^ distance) for i in range(devices)])


def gather_stage(values, stride, size):
    received = {k: swap(values, k * stride) for k in range(size - 1, 0, -1)}
    return [values] + [received[k] for k in range(1, size)]


def rotate(values, cosine, signed_sine):
    return values * cosine + pltpu.roll(values, HD // 2, 1) * signed_sine


def split_pair(values):
    high = values.astype(BF).astype(F32)
    return high, (values - high).astype(BF).astype(F32)


def attend_kernel(layout, heads, kv_heads, *refs):
    (live_ref, place_ref, even_ref, odd_ref, key_ref, value_ref, cos_ref, sin_ref, token_ref, cache_k, cache_v) = refs[:11]
    outputs = refs[11:]
    queries = (even_ref, odd_ref)
    half_rows = even_ref.shape[0]
    share, slots = key_ref.shape[0], cache_k.shape[1]
    group = heads // kv_heads
    scale = HD**-0.5
    own_span, first_token = place_ref[0], place_ref[1]
    own_cos, own_sin = cos_ref[0:share, :], sin_ref[0:share, :]

    def pad(block):
        return jnp.concatenate([block, jnp.zeros((LANES - share, HD), block.dtype)], axis=0).astype(BF)

    nt = (((1,), (1,)), ((), ()))
    for relative, pieces in enumerate(layout):
        span = own_span ^ relative
        rows = sum(size for _, _, size in pieces)
        live = live_ref[span, 0]
        admitted = lax.broadcasted_iota(jnp.int32, (group * rows, slots), 1) < live
        cos = jnp.concatenate([cos_ref[side * half_rows + start : side * half_rows + start + size, :] for side, start, size in pieces], axis=0)
        sin = jnp.concatenate([sin_ref[side * half_rows + start : side * half_rows + start + size, :] for side, start, size in pieces], axis=0)
        if relative == 0:
            token = jnp.concatenate([token_ref[side * half_rows + start : side * half_rows + start + size, :] for side, start, size in pieces], axis=0)
            offset = jnp.concatenate([token - first_token] * group, axis=0)
            column = lax.broadcasted_iota(jnp.int32, (group * rows, LANES), 1)
            causal = jnp.logical_and(column <= offset, column < share)
        lane = lax.broadcasted_iota(jnp.int32, (rows, LANES), 1)
        stats = jnp.zeros((rows, LANES), F32)
        for g in range(kv_heads):
            stacked = []
            for h in range(g * group, (g + 1) * group):
                lanes = slice(h * HD, (h + 1) * HD)
                block = jnp.concatenate([queries[side][start : start + size, lanes].astype(F32) for side, start, size in pieces], axis=0)
                stacked.append(rotate(block, cos, sin).astype(BF))
            query = jnp.concatenate(stacked, axis=0)
            lanes = slice(g * HD, (g + 1) * HD)
            scores = lax.dot_general(query, cache_k[span, :, lanes], nt, preferred_element_type=F32) * scale
            scores = jnp.where(admitted, scores, NEG_FILL)
            top = jnp.max(scores, axis=1, keepdims=True)
            if relative == 0:
                own_key = pad(rotate(key_ref[:, lanes].astype(F32), own_cos, own_sin))
                own_scores = lax.dot_general(query, own_key, nt, preferred_element_type=F32) * scale
                own_scores = jnp.where(causal, own_scores, NEG_FILL)
                top = jnp.maximum(top, jnp.max(own_scores, axis=1, keepdims=True))
            top_high, top_low = split_pair(jnp.maximum(top, MAX_FLOOR))
            top = top_high + top_low
            weights = jnp.exp(scores - top)
            total = jnp.sum(weights, axis=1, keepdims=True)
            summed = jnp.dot(weights.astype(BF), cache_v[span, :, lanes], preferred_element_type=F32)
            if relative == 0:
                own_weights = jnp.exp(own_scores - top)
                total = total + jnp.sum(own_weights, axis=1, keepdims=True)
                own_value = pad(value_ref[:, lanes].astype(F32))
                summed = summed + jnp.dot(own_weights.astype(BF), own_value, preferred_element_type=F32)
            total_high, total_low = split_pair(total)
            for index in range(group):
                h = g * group + index
                part = slice(index * rows, (index + 1) * rows)
                for place, column_values in enumerate((top_high, top_low, total_high, total_low)):
                    stats = jnp.where(lane == place * heads + h, column_values[part], stats)
                at = 0
                for side, start, size in pieces:
                    outputs[side][start : start + size, h * HD : (h + 1) * HD] = summed[index * rows + at : index * rows + at + size].astype(BF)
                    at += size
        at = 0
        for side, start, size in pieces:
            outputs[side][start : start + size, heads * HD :] = stats[at : at + size].astype(BF)
            at += size


def attend(layout, heads, kv_heads, live, place, even, odd, keys, values, cos, sin, token, cache_k, cache_v):
    vmem = pl.BlockSpec(memory_space=pltpu.VMEM)
    smem = pl.BlockSpec(memory_space=pltpu.SMEM)
    rows = even.shape[0]
    shape = jax.ShapeDtypeStruct((rows, heads * HD + LANES), BF)
    slots = cache_k.shape[1]
    return pl.pallas_call(
        functools.partial(attend_kernel, layout, heads, kv_heads),
        out_shape=(shape, shape),
        in_specs=[smem, smem] + [vmem] * 9,
        out_specs=(vmem, vmem),
        cost_estimate=pl.CostEstimate(
            flops=8 * rows * heads * HD * slots,
            bytes_accessed=4 * cache_k.size + 8 * rows * heads * HD,
            transcendentals=2 * rows * heads * slots,
        ),
        name="attend",
    )(live, place, even, odd, keys, values, cos, sin, token, cache_k, cache_v)


def merge_kernel(count, heads, last, *refs):
    parts, outputs = refs[:count], refs[count:]
    piece = outputs[0].shape[0]
    width = heads * HD
    for index, out in enumerate(outputs):
        rows = slice(index * piece, (index + 1) * piece)
        tops, totals = [], []
        for part in parts:
            stats = part[rows, width:].astype(F32)
            pair = stats + pltpu.roll(stats, LANES - heads, 1)
            tops.append(pair)
            totals.append(pltpu.roll(pair, LANES - 2 * heads, 1))
        top = functools.reduce(jnp.maximum, tops)
        factors = [jnp.exp(own - top) for own in tops]
        total = functools.reduce(jnp.add, [f * t for f, t in zip(factors, totals)])
        if last:
            inverse = 1.0 / total
            factors = [f * inverse for f in factors]
        for h in range(heads):
            lanes = slice(h * HD, (h + 1) * HD)
            summed = functools.reduce(
                jnp.add, [f[:, h : h + 1] * part[rows, lanes].astype(F32) for f, part in zip(factors, parts)]
            )
            out[:, lanes] = summed.astype(BF)
        if not last:
            lane = lax.broadcasted_iota(jnp.int32, top.shape, 1)
            top_high, top_low = split_pair(top)
            total_high, total_low = split_pair(total)
            packed = jnp.zeros_like(top)
            for place, values in enumerate((top_high, top_low, total_high, total_low)):
                moved = pltpu.roll(values, place * heads, 1) if place else values
                packed = jnp.where(lane // heads == place, moved, packed)
            out[:, width:] = packed.astype(BF)


def merge(parts, pieces, heads, last=False):
    rows = parts[0].shape[0]
    width = heads * HD + (0 if last else LANES)
    shape = jax.ShapeDtypeStruct((rows // pieces, width), BF)
    vmem = pl.BlockSpec(memory_space=pltpu.VMEM)
    return pl.pallas_call(
        functools.partial(merge_kernel, len(parts), heads, last),
        out_shape=(shape,) * pieces,
        in_specs=[vmem] * len(parts),
        out_specs=(vmem,) * pieces,
        cost_estimate=pl.CostEstimate(
            flops=4 * len(parts) * rows * heads * HD,
            bytes_accessed=2 * (len(parts) + 1) * rows * width,
            transcendentals=len(parts) * rows * LANES,
        ),
        name="merge",
    )(*parts)


def per_device(query_in, key_in, value_in, cache_keys, cache_values, live_slots, span_starts):
    devices = lax.axis_size("kv")
    me = lax.axis_index("kv")
    share = query_in.shape[0]
    span_count = span_starts.shape[0]
    span_len = share * devices // span_count
    per_span = devices // span_count
    heads = query_in.shape[1] // HD
    kv_heads = key_in.shape[1] // HD
    (outer_stride, outer), (inner_stride, inner), (core_stride, core) = stages_of(devices)

    order = [
        o * outer_stride + i * inner_stride + c * core_stride for c in range(core) for i in range(inner) for o in range(outer)
    ]
    half_rows = share * outer * inner
    layout = [[] for _ in range(span_count)]
    for index, distance in enumerate(order):
        row = index * share
        pieces = layout[distance // per_span]
        side, start = divmod(row, half_rows)
        if pieces and pieces[-1][0] == side and pieces[-1][1] + pieces[-1][2] == start:
            pieces[-1] = (side, pieces[-1][1], pieces[-1][2] + share)
        else:
            pieces.append((side, start, share))

    owner = me ^ np.repeat(np.asarray(order, np.int32), share)
    token = owner * share + np.tile(np.arange(share, dtype=np.int32), devices)
    span = token // span_len
    start = functools.reduce(
        lambda found, index: jnp.where(span == index, span_starts[index], found), range(1, span_count), span_starts[0]
    )
    positions = start + token % span_len
    turns = turn_table(HD)
    phases = positions[:, None] * np.concatenate([turns, turns])[None, :]
    angles = phases.astype(F32) * (2.0 * np.pi / 2.0**32)
    sign = np.repeat(np.asarray([-1.0, 1.0], np.float32), HD // 2)
    cos, sin = jnp.cos(angles), jnp.sin(angles) * sign[None, :]

    rows = jnp.concatenate(gather_stage(query_in, outer_stride, outer), axis=0)
    rows = jnp.concatenate(gather_stage(rows, inner_stride, inner), axis=0)
    even, odd = gather_stage(rows, core_stride, core)

    place = jnp.stack([me * share // span_len, me * share]).astype(jnp.int32)
    even, odd = attend(
        layout, heads, kv_heads, live_slots, place, even, odd, key_in, value_in, cos, sin, token[:, None], cache_keys, cache_values
    )
    kept = merge((even, swap(odd, core_stride)), inner, heads)
    received = [swap(kept[k], k * inner_stride) for k in range(inner - 1, 0, -1)]
    kept = merge([kept[0]] + received, outer, heads)
    received = [swap(kept[k], k * outer_stride) for k in range(outer - 1, 0, -1)]
    (attended,) = merge([kept[0]] + received, 1, heads, last=True)
    return attended


def solution(mesh):
    in_specs = (
        P(("groups", "kv"), None),
        P(("groups", "kv"), None),
        P(("groups", "kv"), None),
        P("groups", "kv", None),
        P("groups", "kv", None),
        P("groups", "kv"),
        P("groups"),
    )
    out_specs = P(("groups", "kv"), None)
    return jax.shard_map(per_device, mesh=mesh, in_specs=in_specs, out_specs=out_specs, check_vma=False)
```

```python
import functools

import jax
import jax.numpy as jnp
import numpy as np
from jax import lax
from jax.experimental import pallas as pl
from jax.experimental.pallas import tpu as pltpu
from jax.sharding import PartitionSpec as P

HD = 128
LANES = 128
NEG_FILL = -1e30
MAX_FLOOR = -5e29
BF = jnp.bfloat16
F32 = jnp.float32


def turn_table(head_size):
    half_size = head_size // 2
    frequency = 500000.0 ** (-np.arange(half_size) * 2.0 / head_size)
    turn_counts = np.floor(frequency / (2.0 * np.pi) * 2.0**32 + 0.5).astype(np.int64) % 2**32
    turn_counts = np.where(turn_counts >= 2**31, turn_counts - 2**32, turn_counts)
    return turn_counts.astype(np.int32)


def stages_of(devices):
    core = 2 if devices % 2 == 0 else 1
    rest = devices // core
    inner = 1 << ((rest.bit_length() - 1) // 2)
    outer = rest // inner
    return (core * inner, outer), (core, inner), (1, core)


def swap(values, distance):
    devices = lax.axis_size("kv")
    return lax.ppermute(values, "kv", [(i, i ^ distance) for i in range(devices)])


def gather_stage(values, stride, size):
    received = {k: swap(values, k * stride) for k in range(size - 1, 0, -1)}
    return [values] + [received[k] for k in range(1, size)]


def rotate(values, cosine, signed_sine):
    return values * cosine + pltpu.roll(values, HD // 2, 1) * signed_sine


def split_pair(values):
    high = values.astype(BF).astype(F32)
    return high, (values - high).astype(BF).astype(F32)


def split_index(values, size):
    if size & (size - 1) == 0:
        return values >> (size.bit_length() - 1), values & (size - 1)
    quotient = lax.div(values, jnp.int32(size))
    return quotient, values - quotient * size


def prepare_kernel(share, span_len, stages, me_ref, start_ref, turn_ref, cos_ref, sin_ref, token_ref):
    (outer_stride, outer), (inner_stride, inner), (core_stride, core) = stages
    spans = start_ref.shape[0]
    me = me_ref[0]
    row = lax.broadcasted_iota(jnp.int32, cos_ref.shape, 0)
    relative, rest = split_index(row, cos_ref.shape[0] // spans)
    side, rest = split_index(rest, cos_ref.shape[0] // spans // core)
    member, within = split_index(rest, share)
    high, low = split_index(member, inner)
    distance = (relative * (outer // spans) + high) * outer_stride + low * inner_stride + side * core_stride
    token = (me ^ distance) * share + within
    span, step = split_index(token, span_len)
    start = jnp.full(cos_ref.shape, start_ref[0], jnp.int32)
    for index in range(1, spans):
        start = jnp.where(span == index, start_ref[index], start)
    phases = (start + step) * turn_ref[...]
    angles = phases.astype(F32) * (2.0 * np.pi / 2.0**32)
    lane = lax.broadcasted_iota(jnp.int32, cos_ref.shape, 1)
    cos_ref[...] = jnp.cos(angles)
    sine = jnp.sin(angles)
    sin_ref[...] = jnp.where(lane < HD // 2, -sine, sine)
    token_ref[...] = token


def prepare(rows, share, span_len, stages, me, starts):
    vmem = pl.BlockSpec(memory_space=pltpu.VMEM)
    smem = pl.BlockSpec(memory_space=pltpu.SMEM)
    turns = turn_table(HD)
    turns = jnp.asarray(np.concatenate([turns, turns])[None, :])
    table = jax.ShapeDtypeStruct((rows, HD), F32)
    return pl.pallas_call(
        functools.partial(prepare_kernel, share, span_len, stages),
        out_shape=(table, table, jax.ShapeDtypeStruct((rows, HD), jnp.int32)),
        in_specs=[smem, smem, vmem],
        out_specs=(vmem, vmem, vmem),
        cost_estimate=pl.CostEstimate(flops=100 * rows * HD, bytes_accessed=12 * rows * HD, transcendentals=2 * rows * HD),
        compiler_params=pltpu.CompilerParams(vmem_limit_bytes=4 << 20),
        name="prepare",
    )(me, starts, turns)


def attend_kernel(sources, heads, kv_heads, span_len, *refs):
    (me_ref, live_ref, even_ref, odd_ref, key_ref, value_ref, cos_ref, sin_ref, token_ref, cache_k, cache_v) = refs[:11]
    outputs = refs[11:]
    queries = (even_ref, odd_ref)[: len(outputs)]
    share, slots = key_ref.shape[0], cache_k.shape[1]
    spans = cache_k.shape[0]
    group = heads // kv_heads
    scale = HD**-0.5
    first_token = me_ref[0] * share
    own_span, _ = split_index(first_token, span_len)
    own_cos, own_sin = cos_ref[0:share, :], sin_ref[0:share, :]
    side_rows = even_ref.shape[0] // spans
    rows = side_rows * len(outputs)

    def pad(block):
        return jnp.concatenate([block, jnp.zeros((LANES - share, HD), block.dtype)], axis=0).astype(BF)

    nt = (((1,), (1,)), ((), ()))
    for relative in range(spans):
        span = own_span ^ relative
        table = slice(relative * rows, (relative + 1) * rows)
        admitted = lax.broadcasted_iota(jnp.int32, (group * rows, slots), 1) < live_ref[span]
        cos, sin = cos_ref[table, :], sin_ref[table, :]
        if relative == 0:
            offset = jnp.concatenate([token_ref[table, :] - first_token] * group, axis=0)
            column = lax.broadcasted_iota(jnp.int32, (group * rows, LANES), 1)
            causal = jnp.logical_and(column <= offset, column < share)
        lane = lax.broadcasted_iota(jnp.int32, (rows, LANES), 1)
        stats = jnp.zeros((rows, LANES), F32)
        for g in range(kv_heads):
            stacked = []
            for h in range(g * group, (g + 1) * group):
                lanes = slice(h * HD, (h + 1) * HD)
                block = jnp.concatenate(
                    [side[at : at + share, lanes].astype(F32) for side in queries for at in sources[relative]], axis=0
                )
                stacked.append(rotate(block, cos, sin).astype(BF))
            query = jnp.concatenate(stacked, axis=0)
            lanes = slice(g * HD, (g + 1) * HD)
            scores = lax.dot_general(query, cache_k[span, :, lanes], nt, preferred_element_type=F32) * scale
            scores = jnp.where(admitted, scores, NEG_FILL)
            top = jnp.max(scores, axis=1, keepdims=True)
            if relative == 0:
                own_key = pad(rotate(key_ref[:, lanes].astype(F32), own_cos, own_sin))
                own_scores = lax.dot_general(query, own_key, nt, preferred_element_type=F32) * scale
                own_scores = jnp.where(causal, own_scores, NEG_FILL)
                top = jnp.maximum(top, jnp.max(own_scores, axis=1, keepdims=True))
            top_high, top_low = split_pair(jnp.maximum(top, MAX_FLOOR))
            top = top_high + top_low
            weights = jnp.exp(scores - top)
            total = jnp.sum(weights, axis=1, keepdims=True)
            summed = jnp.dot(weights.astype(BF), cache_v[span, :, lanes], preferred_element_type=F32)
            if relative == 0:
                own_weights = jnp.exp(own_scores - top)
                total = total + jnp.sum(own_weights, axis=1, keepdims=True)
                own_value = pad(value_ref[:, lanes].astype(F32))
                summed = summed + jnp.dot(own_weights.astype(BF), own_value, preferred_element_type=F32)
            total_high, total_low = split_pair(total)
            for index in range(group):
                h = g * group + index
                part = slice(index * rows, (index + 1) * rows)
                for place, values in enumerate((top_high, top_low, total_high, total_low)):
                    stats = jnp.where(lane == place * heads + h, values[part], stats)
                for side, out in enumerate(outputs):
                    at = index * rows + side * side_rows
                    out[relative * side_rows : (relative + 1) * side_rows, h * HD : (h + 1) * HD] = summed[
                        at : at + side_rows
                    ].astype(BF)
        for side, out in enumerate(outputs):
            out[relative * side_rows : (relative + 1) * side_rows, heads * HD :] = stats[
                side * side_rows : (side + 1) * side_rows
            ].astype(BF)


def attend(sources, heads, kv_heads, span_len, me, live, sides, keys, values, tables, cache_k, cache_v):
    vmem = pl.BlockSpec(memory_space=pltpu.VMEM)
    smem = pl.BlockSpec(memory_space=pltpu.SMEM)
    rows, slots = sides[0].shape[0], cache_k.shape[1]
    shape = jax.ShapeDtypeStruct((rows, heads * HD + LANES), BF)
    return pl.pallas_call(
        functools.partial(attend_kernel, sources, heads, kv_heads, span_len),
        out_shape=(shape,) * len(sides),
        in_specs=[smem, smem] + [vmem] * 9,
        out_specs=(vmem,) * len(sides),
        cost_estimate=pl.CostEstimate(
            flops=8 * rows * heads * HD * slots,
            bytes_accessed=4 * cache_k.size + 8 * rows * heads * HD,
            transcendentals=2 * rows * heads * slots,
        ),
        compiler_params=pltpu.CompilerParams(vmem_limit_bytes=16 << 20),
        name="attend",
    )(me, live, *sides, keys, values, *tables, cache_k, cache_v)


def merge_kernel(count, heads, last, *refs):
    parts, outputs = refs[:count], refs[count:]
    piece = outputs[0].shape[0]
    width = heads * HD
    for index, out in enumerate(outputs):
        rows = slice(index * piece, (index + 1) * piece)
        tops, totals = [], []
        for part in parts:
            stats = part[rows, width:].astype(F32)
            pair = stats + pltpu.roll(stats, LANES - heads, 1)
            tops.append(pair)
            totals.append(pltpu.roll(pair, LANES - 2 * heads, 1))
        top = functools.reduce(jnp.maximum, tops)
        factors = [jnp.exp(own - top) for own in tops]
        total = functools.reduce(jnp.add, [f * t for f, t in zip(factors, totals)])
        if last:
            inverse = 1.0 / total
            factors = [f * inverse for f in factors]
        for h in range(heads):
            lanes = slice(h * HD, (h + 1) * HD)
            summed = functools.reduce(
                jnp.add, [f[:, h : h + 1] * part[rows, lanes].astype(F32) for f, part in zip(factors, parts)]
            )
            out[:, lanes] = summed.astype(BF)
        if not last:
            lane = lax.broadcasted_iota(jnp.int32, top.shape, 1)
            top_high, top_low = split_pair(top)
            total_high, total_low = split_pair(total)
            packed = jnp.zeros_like(top)
            for place, values in enumerate((top_high, top_low, total_high, total_low)):
                moved = pltpu.roll(values, place * heads, 1) if place else values
                packed = jnp.where(lane // heads == place, moved, packed)
            out[:, width:] = packed.astype(BF)


def merge(parts, pieces, heads, last=False):
    rows = parts[0].shape[0]
    width = heads * HD + (0 if last else LANES)
    shape = jax.ShapeDtypeStruct((rows // pieces, width), BF)
    vmem = pl.BlockSpec(memory_space=pltpu.VMEM)
    return pl.pallas_call(
        functools.partial(merge_kernel, len(parts), heads, last),
        out_shape=(shape,) * pieces,
        in_specs=[vmem] * len(parts),
        out_specs=(vmem,) * pieces,
        cost_estimate=pl.CostEstimate(
            flops=4 * len(parts) * rows * heads * HD,
            bytes_accessed=2 * (len(parts) + 1) * rows * width,
            transcendentals=len(parts) * rows * LANES,
        ),
        compiler_params=pltpu.CompilerParams(vmem_limit_bytes=4 << 20),
        name="merge",
    )(*parts)


def per_device(query_in, key_in, value_in, cache_keys, cache_values, live_slots, span_starts):
    devices = lax.axis_size("kv")
    me = lax.axis_index("kv")
    share = query_in.shape[0]
    span_count = span_starts.shape[0]
    span_len = share * devices // span_count
    heads = query_in.shape[1] // HD
    kv_heads = key_in.shape[1] // HD
    stages = stages_of(devices)
    (outer_stride, outer), (inner_stride, inner), (core_stride, core) = stages
    place = me.reshape(1)
    tables = prepare(share * devices, share, span_len, stages, place, span_starts)

    rows = jnp.concatenate(gather_stage(query_in, outer_stride, outer), axis=0)
    rows = jnp.concatenate(gather_stage(rows, inner_stride, inner), axis=0)
    sides = gather_stage(rows, core_stride, core)

    per_span = outer // span_count
    sources = [
        [(i * outer + o) * share for o in range(s * per_span, (s + 1) * per_span) for i in range(inner)]
        for s in range(span_count)
    ]
    live = live_slots.reshape(span_count)
    even, odd = attend(sources, heads, kv_heads, span_len, place, live, sides, key_in, value_in, tables, cache_keys, cache_values)
    kept = merge((even, swap(odd, core_stride)), outer, heads)
    received = [swap(kept[k], k * outer_stride) for k in range(outer - 1, 0, -1)]
    kept = merge([kept[0]] + received, inner, heads)
    received = [swap(kept[k], k * inner_stride) for k in range(inner - 1, 0, -1)]
    (attended,) = merge([kept[0]] + received, 1, heads, last=True)
    return attended


def solution(mesh):
    in_specs = (
        P(("groups", "kv"), None),
        P(("groups", "kv"), None),
        P(("groups", "kv"), None),
        P("groups", "kv", None),
        P("groups", "kv", None),
        P("groups", "kv"),
        P("groups"),
    )
    out_specs = P(("groups", "kv"), None)
    return jax.shard_map(per_device, mesh=mesh, in_specs=in_specs, out_specs=out_specs, check_vma=False)
```

```python
import functools

import jax
import jax.numpy as jnp
import numpy as np
from jax import lax
from jax.experimental import pallas as pl
from jax.experimental.pallas import tpu as pltpu
from jax.sharding import PartitionSpec as P


HD = 128
LANES = 128
NEG_FILL = -1e30
MAX_FLOOR = -5e29
LOG2E = 1.4426950408889634
PREPARE_FLOPS = 10_000_000_000
BF = jnp.bfloat16
F32 = jnp.float32


def turn_table(head_size):
    half_size = head_size // 2
    frequency = 500000.0 ** (-np.arange(half_size) * 2.0 / head_size)
    turn_counts = np.floor(frequency / (2.0 * np.pi) * 2.0**32 + 0.5).astype(np.int64) % 2**32
    turn_counts = np.where(turn_counts >= 2**31, turn_counts - 2**32, turn_counts)
    return turn_counts.astype(np.int32)


def stages_of(devices):
    core = 2 if devices % 2 == 0 else 1
    rest = devices // core
    inner = 1 << ((rest.bit_length() - 1) // 2)
    outer = rest // inner
    return (core * inner, outer), (core, inner), (1, core)


def swap(values, distance):
    devices = lax.axis_size("kv")
    return lax.ppermute(values, "kv", [(i, i ^ distance) for i in range(devices)])


def rotate(values, cosine, signed_sine):
    return values * cosine + pltpu.roll(values, HD // 2, 1) * signed_sine


def split_pair(values):
    high = values.astype(BF).astype(F32)
    return high, (values - high).astype(BF).astype(F32)


def split_index(values, size):
    if size & (size - 1) == 0:
        return values >> (size.bit_length() - 1), values & (size - 1)
    quotient = lax.div(values, jnp.int32(size))
    return quotient, values - quotient * size


def prepare_kernel(share, span_len, stages, *refs):
    (live_ref, start_ref, turn_ref, query_in, key_in, query_out, key_out, cos_ref, sin_ref, offset_ref, limit_ref) = refs
    (outer_stride, outer), (inner_stride, inner), (core_stride, core) = stages
    spans = live_ref.shape[0]
    me = lax.axis_index("kv")
    own_span, _ = split_index(me * share, span_len)
    query_out[...] = query_in[...]
    for relative in range(spans):
        limit_ref[relative : relative + 1, :] = jnp.full((1, LANES), live_ref[own_span ^ relative], jnp.int32)
    row = lax.broadcasted_iota(jnp.int32, cos_ref.shape, 0)
    member, within = split_index(row, share)
    member, high = split_index(member, outer)
    side, low = split_index(member, inner)
    distance = high * outer_stride + low * inner_stride + side * core_stride
    token = (me ^ distance) * share + within
    span, step = split_index(token, span_len)
    start = jnp.full(cos_ref.shape, start_ref[0], jnp.int32)
    for index in range(1, spans):
        start = jnp.where(span == index, start_ref[index], start)
    phases = (start + step) * turn_ref[...]
    angles = phases.astype(F32) * (2.0 * np.pi / 2.0**32)
    lane = lax.broadcasted_iota(jnp.int32, cos_ref.shape, 1)
    cos_ref[...] = jnp.cos(angles)
    sine = jnp.sin(angles)
    sin_ref[...] = jnp.where(lane < HD // 2, -sine, sine)
    offset_ref[...] = token - me * share
    for g in range(key_in.shape[1] // HD):
        lanes = slice(g * HD, (g + 1) * HD)
        key_out[:, lanes] = rotate(key_in[:, lanes].astype(F32), cos_ref[0:share, :], sin_ref[0:share, :]).astype(BF)


def prepare(span_len, stages, live, starts, query_in, key_in):
    vmem = pl.BlockSpec(memory_space=pltpu.VMEM)
    smem = pl.BlockSpec(memory_space=pltpu.SMEM)
    share = query_in.shape[0]
    rows = share * stages[0][1] * stages[1][1] * stages[2][1]
    spans = live.shape[0]
    turns = turn_table(HD)
    turns = jnp.asarray(np.concatenate([turns, turns])[None, :])
    like = [jax.ShapeDtypeStruct(array.shape, array.dtype) for array in (query_in, key_in)]
    table = jax.ShapeDtypeStruct((rows, HD), F32)
    return pl.pallas_call(
        functools.partial(prepare_kernel, share, span_len, stages),
        out_shape=(
            *like,
            table,
            table,
            jax.ShapeDtypeStruct((rows, HD), jnp.int32),
            jax.ShapeDtypeStruct((spans, LANES), jnp.int32),
        ),
        in_specs=[smem, smem, vmem, vmem, vmem],
        out_specs=(vmem,) * 6,
        cost_estimate=pl.CostEstimate(flops=PREPARE_FLOPS, bytes_accessed=12 * rows * HD, transcendentals=2 * rows * HD),
        compiler_params=pltpu.CompilerParams(vmem_limit_bytes=4 << 20),
        name="prepare",
    )(live, starts, turns, query_in, key_in)


def attend_kernel(blocks, heads, kv_heads, span_len, *refs):
    count = len(blocks)
    queries = refs[:count]
    (key_ref, cos_ref, sin_ref, offset_ref, limit_ref, value_ref, cache_k, cache_v) = refs[count : count + 8]
    outputs = refs[count + 8 :]
    share, slots = key_ref.shape[0], cache_k.shape[1]
    spans = cache_k.shape[0]
    group = heads // kv_heads
    scale = HD**-0.5 * LOG2E
    piece = queries[0].shape[0] // spans
    rows = piece * count
    own_span, _ = split_index(lax.axis_index("kv") * share, span_len)

    def pad(block):
        return jnp.concatenate([block.astype(F32), jnp.zeros((LANES - share, HD), F32)], axis=0).astype(BF)

    nt = (((1,), (1,)), ((), ()))
    parts = [slice(relative * piece, (relative + 1) * piece) for relative in range(spans)]
    tables = [
        [slice(block * queries[0].shape[0] + part.start, block * queries[0].shape[0] + part.stop) for block in blocks]
        for part in parts
    ]
    cells = [(relative, g) for relative in range(spans) for g in range(kv_heads)]
    slot = lax.broadcasted_iota(jnp.int32, (1, slots), 1)
    limits = [jnp.concatenate([limit_ref[part : part + 1, :]] * (slots // LANES), axis=1) for part in range(spans)]
    biases = [jnp.where(slot < limit, 0.0, NEG_FILL) for limit in limits]
    offset = jnp.concatenate([offset_ref[table, :] for table in tables[0]], axis=0)
    column = lax.broadcasted_iota(jnp.int32, (rows, LANES), 1)
    own_bias = jnp.where(jnp.logical_and(column <= offset, column < share), 0.0, NEG_FILL)
    own_bias = jnp.concatenate([own_bias] * group, axis=0)
    lane = lax.broadcasted_iota(jnp.int32, (rows, LANES), 1)

    raw, raw_own = {}, {}
    for relative, g in cells:
        stacked = []
        for h in range(g * group, (g + 1) * group):
            lanes = slice(h * HD, (h + 1) * HD)
            for source, table in zip(queries, tables[relative]):
                stacked.append(rotate(source[parts[relative], lanes].astype(F32), cos_ref[table, :], sin_ref[table, :]))
        query = jnp.concatenate(stacked, axis=0).astype(BF)
        lanes = slice(g * HD, (g + 1) * HD)
        raw[relative, g] = lax.dot_general(query, cache_k[own_span ^ relative, :, lanes], nt, preferred_element_type=F32)
        if relative == 0:
            raw_own[g] = lax.dot_general(query, pad(key_ref[:, lanes]), nt, preferred_element_type=F32)

    weights, own_weights, columns = {}, {}, {}
    for relative, g in cells:
        scores = raw[relative, g] * scale + biases[relative]
        top = jnp.max(scores, axis=1, keepdims=True)
        if relative == 0:
            own_scores = raw_own[g] * scale + own_bias
            top = jnp.maximum(top, jnp.max(own_scores, axis=1, keepdims=True))
        top_high, top_low = split_pair(jnp.maximum(top, MAX_FLOOR))
        top = top_high + top_low
        found = jnp.exp2(scores - top)
        total = jnp.sum(found, axis=1, keepdims=True)
        weights[relative, g] = found.astype(BF)
        if relative == 0:
            found = jnp.exp2(own_scores - top)
            total = total + jnp.sum(found, axis=1, keepdims=True)
            own_weights[g] = found.astype(BF)
        columns[relative, g] = (top_high, top_low, *split_pair(total))

    for relative, g in cells:
        lanes = slice(g * HD, (g + 1) * HD)
        summed = jnp.dot(weights[relative, g], cache_v[own_span ^ relative, :, lanes], preferred_element_type=F32)
        if relative == 0:
            summed = summed + jnp.dot(own_weights[g], pad(value_ref[:, lanes]), preferred_element_type=F32)
        for index in range(group):
            h = g * group + index
            for n, out in enumerate(outputs):
                at = index * rows + n * piece
                out[parts[relative], h * HD : (h + 1) * HD] = summed[at : at + piece].astype(BF)

    for relative in range(spans):
        stats = jnp.zeros((rows, LANES), F32)
        for g in range(kv_heads):
            for index in range(group):
                own = slice(index * rows, (index + 1) * rows)
                for place, values in enumerate(columns[relative, g]):
                    stats = jnp.where(lane == place * heads + g * group + index, values[own], stats)
        for n, out in enumerate(outputs):
            out[parts[relative], heads * HD :] = stats[n * piece : (n + 1) * piece].astype(BF)


def attend(blocks, heads, kv_heads, span_len, queries, held):
    vmem = pl.BlockSpec(memory_space=pltpu.VMEM)
    cache_k = held[-1]
    rows, slots = queries[0].shape[0], cache_k.shape[1]
    shape = jax.ShapeDtypeStruct((rows, heads * HD + LANES), BF)
    return pl.pallas_call(
        functools.partial(attend_kernel, blocks, heads, kv_heads, span_len),
        out_shape=(shape,) * len(queries),
        in_specs=[vmem] * (len(queries) + len(held)),
        out_specs=(vmem,) * len(queries),
        cost_estimate=pl.CostEstimate(
            flops=4 * len(queries) * rows * heads * HD * slots,
            bytes_accessed=4 * cache_k.size + 4 * len(queries) * rows * heads * HD,
            transcendentals=len(queries) * rows * heads * slots,
        ),
        compiler_params=pltpu.CompilerParams(vmem_limit_bytes=8 << 20),
        name="attend",
    )(*queries, *held)


def merge_kernel(groups, count, heads, last, *refs):
    outputs = refs[groups * count :]
    width = heads * HD
    sets = [refs[member * count : (member + 1) * count] for member in range(groups)]
    share = outputs[0].shape[0] // groups

    def store(member, lanes, values):
        for index, out in enumerate(outputs):
            out[member * share : (member + 1) * share, lanes] = values[index * share : (index + 1) * share].astype(BF)

    scaled = []
    for member, parts in enumerate(sets):
        pairs = []
        for part in parts:
            stats = part[:, width:].astype(F32)
            pairs.append(stats + pltpu.roll(stats, LANES - heads, 1))
        top = functools.reduce(jnp.maximum, pairs)
        factors = [jnp.exp2(own - top) for own in pairs]
        total = functools.reduce(
            jnp.add, [f * pltpu.roll(pair, LANES - 2 * heads, 1) for f, pair in zip(factors, pairs)]
        )
        if last:
            inverse = 1.0 / total
            factors = [f * inverse for f in factors]
        else:
            lane = lax.broadcasted_iota(jnp.int32, top.shape, 1)
            packed = jnp.zeros_like(top)
            for place, values in enumerate((*split_pair(top), *split_pair(total))):
                moved = pltpu.roll(values, place * heads, 1) if place else values
                packed = jnp.where(lane // heads == place, moved, packed)
            store(member, slice(width, width + LANES), packed)
        scaled.append(factors)
    for h in range(heads):
        lanes = slice(h * HD, (h + 1) * HD)
        for member, parts in enumerate(sets):
            terms = [f[:, h : h + 1] * part[:, lanes].astype(F32) for f, part in zip(scaled[member], parts)]
            store(member, lanes, functools.reduce(jnp.add, terms))


def merge(groups, pieces, heads, last=False):
    rows = groups[0][0].shape[0]
    count = len(groups[0])
    width = heads * HD + (0 if last else LANES)
    shape = jax.ShapeDtypeStruct((len(groups) * rows // pieces, width), BF)
    vmem = pl.BlockSpec(memory_space=pltpu.VMEM)
    total = len(groups) * count
    return pl.pallas_call(
        functools.partial(merge_kernel, len(groups), count, heads, last),
        out_shape=(shape,) * pieces,
        in_specs=[vmem] * total,
        out_specs=(vmem,) * pieces,
        cost_estimate=pl.CostEstimate(
            flops=4 * total * rows * heads * HD,
            bytes_accessed=2 * (total + len(groups)) * rows * width,
            transcendentals=total * rows * LANES,
        ),
        compiler_params=pltpu.CompilerParams(vmem_limit_bytes=4 << 20),
        name="merge",
    )(*[part for group in groups for part in group])


def per_device(query_in, key_in, value_in, cache_keys, cache_values, live_slots, span_starts):
    devices = lax.axis_size("kv")
    share = query_in.shape[0]
    span_count = span_starts.shape[0]
    span_len = share * devices // span_count
    heads = query_in.shape[1] // HD
    kv_heads = key_in.shape[1] // HD
    stages = stages_of(devices)
    (outer_stride, outer), (inner_stride, inner), (core_stride, core) = stages

    arrived = {k: swap(query_in, k * outer_stride) for k in range(1, outer)}
    query_own, *held = prepare(span_len, stages, live_slots.reshape(span_count), span_starts, query_in, key_in)
    held = [*held, value_in, cache_keys, cache_values]
    rows = jnp.concatenate([query_own] + [arrived[k] for k in range(1, outer)], axis=0)
    chunks = [rows] + [swap(rows, i * inner_stride) for i in range(1, inner)]
    groups = []
    for i, chunk in enumerate(chunks):
        other = swap(chunk, core_stride)
        if i == 0:
            even, odd = attend((i, inner + i), heads, kv_heads, span_len, (chunk, other), held)
        else:
            (even,) = attend((i,), heads, kv_heads, span_len, (chunk,), held)
            (odd,) = attend((inner + i,), heads, kv_heads, span_len, (other,), held)
        groups.append((even, swap(odd, core_stride)))
    kept = merge(groups, outer, heads)
    received = [swap(kept[k], k * outer_stride) for k in range(1, outer)]
    kept = merge([[kept[0]] + received], inner, heads)
    received = [swap(kept[k], k * inner_stride) for k in range(1, inner)]
    (attended,) = merge([[kept[0]] + received], 1, heads, last=True)
    return attended


def solution(mesh):
    in_specs = (
        P(("groups", "kv"), None),
        P(("groups", "kv"), None),
        P(("groups", "kv"), None),
        P("groups", "kv", None),
        P("groups", "kv", None),
        P("groups", "kv"),
        P("groups"),
    )
    out_specs = P(("groups", "kv"), None)
    return jax.shard_map(per_device, mesh=mesh, in_specs=in_specs, out_specs=out_specs, check_vma=False)
```

```python
import functools

import jax
import jax.numpy as jnp
import numpy as np
from jax import lax
from jax.experimental import pallas as pl
from jax.experimental.pallas import tpu as pltpu
from jax.sharding import PartitionSpec as P


HD = 128
LANES = 128
NEG_FILL = -1e30
MAX_FLOOR = -5e29
LOG2E = 1.4426950408889634
PREPARE_FLOPS = 10_000_000_000
BF = jnp.bfloat16
F32 = jnp.float32


def turn_table(head_size):
    half_size = head_size // 2
    frequency = 500000.0 ** (-np.arange(half_size) * 2.0 / head_size)
    turn_counts = np.floor(frequency / (2.0 * np.pi) * 2.0**32 + 0.5).astype(np.int64) % 2**32
    turn_counts = np.where(turn_counts >= 2**31, turn_counts - 2**32, turn_counts)
    return turn_counts.astype(np.int32)


def stages_of(devices):
    core = 2 if devices % 2 == 0 else 1
    rest = devices // core
    inner = 1 << ((rest.bit_length() - 1) // 2)
    outer = rest // inner
    return (core * inner, outer), (core, inner), (1, core)


def swap(values, distance):
    devices = lax.axis_size("kv")
    return lax.ppermute(values, "kv", [(i, i ^ distance) for i in range(devices)])


def rotate(values, cosine, signed_sine):
    return values * cosine + pltpu.roll(values, HD // 2, 1) * signed_sine


def split_pair(values):
    high = values.astype(BF).astype(F32)
    return high, (values - high).astype(BF).astype(F32)


def split_index(values, size):
    if size & (size - 1) == 0:
        return values >> (size.bit_length() - 1), values & (size - 1)
    quotient = lax.div(values, jnp.int32(size))
    return quotient, values - quotient * size


def prepare_kernel(share, span_len, stages, live_ref, start_ref, query_in, query_out, cos_ref, sin_ref, offset_ref, limit_ref):
    (outer_stride, outer), (inner_stride, inner), (core_stride, _) = stages
    spans = live_ref.shape[0]
    me = lax.axis_index("kv")
    own_span, _ = split_index(me * share, span_len)
    query_out[...] = query_in[...]
    for relative in range(spans):
        limit_ref[relative : relative + 1, :] = jnp.full((1, LANES), live_ref[own_span ^ relative], jnp.int32)
    lane = lax.broadcasted_iota(jnp.int32, (1, HD), 1)
    pair = jnp.where(lane < HD // 2, lane, lane - HD // 2)
    turns = jnp.zeros((1, HD), jnp.int32)
    for index, turn in enumerate(turn_table(HD)):
        turns = jnp.where(pair == index, jnp.int32(turn), turns)
    row = lax.broadcasted_iota(jnp.int32, cos_ref.shape, 0)
    member, within = split_index(row, share)
    low, high = split_index(member, outer)
    distance = jnp.where(low < inner, high * outer_stride + low * inner_stride, core_stride)
    token = (me ^ distance) * share + within
    span, step = split_index(token, span_len)
    start = jnp.full(cos_ref.shape, start_ref[0], jnp.int32)
    for index in range(1, spans):
        start = jnp.where(span == index, start_ref[index], start)
    angles = ((start + step) * turns).astype(F32) * (2.0 * np.pi / 2.0**32)
    cos_ref[...] = jnp.cos(angles)
    sine = jnp.sin(angles)
    sin_ref[...] = jnp.where(lane < HD // 2, -sine, sine)
    offset_ref[...] = token - me * share


def prepare(span_len, stages, live, starts, query_in):
    vmem = pl.BlockSpec(memory_space=pltpu.VMEM)
    smem = pl.BlockSpec(memory_space=pltpu.SMEM)
    share = query_in.shape[0]
    rows = share * (stages[0][1] * stages[1][1] + 1)
    spans = live.shape[0]
    table = jax.ShapeDtypeStruct((rows, HD), F32)
    whole = jax.ShapeDtypeStruct((rows, HD), jnp.int32)
    limits = jax.ShapeDtypeStruct((spans, LANES), jnp.int32)
    return pl.pallas_call(
        functools.partial(prepare_kernel, share, span_len, stages),
        out_shape=(jax.ShapeDtypeStruct(query_in.shape, BF), table, table, whole, limits),
        in_specs=[smem, smem, vmem],
        out_specs=(vmem,) * 5,
        cost_estimate=pl.CostEstimate(flops=PREPARE_FLOPS, bytes_accessed=12 * rows * HD, transcendentals=2 * rows * HD),
        compiler_params=pltpu.CompilerParams(vmem_limit_bytes=4 << 20),
        name="prepare",
    )(live, starts, query_in)


def attend_kernel(chunk, outer, core, core_stride, heads, kv_heads, span_len, earlier, *refs):
    query_ref, refs = refs[0], refs[1:]
    before, refs = refs[:earlier], refs[earlier:]
    (cos_ref, sin_ref, offset_ref), refs = refs[:3], refs[3:]
    sides = [refs[side * 5 : side * 5 + 5] for side in range(core)]
    outputs = refs[5 * core :]
    _, key_ref, _, cache_k, _ = sides[0]
    share, slots, spans = key_ref.shape[0], cache_k.shape[1], cache_k.shape[0]
    group = heads // kv_heads
    scale = HD**-0.5 * LOG2E
    total_rows = query_ref.shape[0]
    rows = total_rows // spans
    me = lax.axis_index("kv")
    own_span, _ = split_index(me * share, span_len)
    key_rows = [slice(0, share), slice(cos_ref.shape[0] - share, cos_ref.shape[0])]
    nt = (((1,), (1,)), ((), ()))
    cells = [(relative, g) for relative in range(spans) for g in range(kv_heads)]
    slot = lax.broadcasted_iota(jnp.int32, (1, slots), 1)
    biases = {}
    for relative in range(spans):
        for side in range(core):
            limit = jnp.concatenate([sides[side][0][relative : relative + 1, :]] * (slots // LANES), axis=1)
            biases[relative, side] = jnp.where(slot < limit, 0.0, NEG_FILL)
    lane = lax.broadcasted_iota(jnp.int32, (rows, LANES), 1)
    other = ((me ^ core_stride) - me) * share - share
    place = jnp.where(lane < share, lane, lane + other)
    offset = offset_ref[chunk * total_rows : chunk * total_rows + rows, :]
    admitted = jnp.logical_and(place <= offset, lane < core * share)
    own_bias = jnp.concatenate([jnp.where(admitted, 0.0, NEG_FILL)] * group, axis=0)

    def stack_new(blocks):
        filler = jnp.zeros((LANES - core * share, HD), F32)
        return jnp.concatenate([*blocks, filler], axis=0).astype(BF)

    raw, raw_own = {}, {}
    for relative, g in cells:
        span = own_span ^ relative
        part = slice(relative * rows, (relative + 1) * rows)
        table = slice(chunk * total_rows + relative * rows, chunk * total_rows + (relative + 1) * rows)
        cos, sin = cos_ref[table, :], sin_ref[table, :]
        stacked = []
        for h in range(g * group, (g + 1) * group):
            stacked.append(rotate(query_ref[part, h * HD : (h + 1) * HD].astype(F32), cos, sin))
        query = jnp.concatenate(stacked, axis=0).astype(BF)
        lanes = slice(g * HD, (g + 1) * HD)
        for side in range(core):
            raw[relative, g, side] = lax.dot_general(
                query, sides[side][3][span, :, lanes], nt, preferred_element_type=F32
            )
        if relative == 0:
            keys = stack_new(
                [
                    rotate(sides[side][1][:, lanes].astype(F32), cos_ref[key_rows[side], :], sin_ref[key_rows[side], :])
                    for side in range(core)
                ]
            )
            raw_own[g] = lax.dot_general(query, keys, nt, preferred_element_type=F32)

    weights, columns = {}, {}
    for relative, g in cells:
        scores = [raw[relative, g, side] * scale + biases[relative, side] for side in range(core)]
        if relative == 0:
            scores.append(raw_own[g] * scale + own_bias)
        top = functools.reduce(jnp.maximum, [jnp.max(values, axis=1, keepdims=True) for values in scores])
        top_high, top_low = split_pair(jnp.maximum(top, MAX_FLOOR))
        top = top_high + top_low
        found = [jnp.exp2(values - top) for values in scores]
        total = functools.reduce(jnp.add, [jnp.sum(values, axis=1, keepdims=True) for values in found])
        weights[relative, g] = [values.astype(BF) for values in found]
        columns[relative, g] = (top_high, top_low, *split_pair(total))

    def store(relative, lanes, values):
        if len(outputs) == 1:
            outputs[0][relative * rows : (relative + 1) * rows, lanes] = values.astype(BF)
        else:
            for index in range(outer // spans):
                outputs[relative * outer // spans + index][earlier * share : (earlier + 1) * share, lanes] = values[
                    index * share : (index + 1) * share
                ].astype(BF)

    for relative, g in cells:
        span = own_span ^ relative
        lanes = slice(g * HD, (g + 1) * HD)
        terms = [
            jnp.dot(weights[relative, g][side], sides[side][4][span, :, lanes], preferred_element_type=F32)
            for side in range(core)
        ]
        if relative == 0:
            values = stack_new([sides[side][2][:, lanes].astype(F32) for side in range(core)])
            terms.append(jnp.dot(weights[relative, g][core], values, preferred_element_type=F32))
        summed = functools.reduce(jnp.add, terms)
        for index in range(group):
            h = g * group + index
            store(relative, slice(h * HD, (h + 1) * HD), summed[index * rows : (index + 1) * rows])

    for relative in range(spans):
        stats = jnp.zeros((rows, LANES), F32)
        for g in range(kv_heads):
            for index in range(group):
                own = slice(index * rows, (index + 1) * rows)
                for place, values in enumerate(columns[relative, g]):
                    stats = jnp.where(lane == place * heads + g * group + index, values[own], stats)
        store(relative, slice(heads * HD, heads * HD + LANES), stats)
    for index, source in enumerate(before):
        for high, out in enumerate(outputs):
            out[index * share : (index + 1) * share, :] = (
                source[high * share : (high + 1) * share, :].astype(F32).astype(BF)
            )


def attend(chunk, stages, heads, kv_heads, span_len, query, before, tables, sides, last):
    vmem = pl.BlockSpec(memory_space=pltpu.VMEM)
    (_, outer), _, (core_stride, core) = stages
    rows, slots = query.shape[0], sides[0][3].shape[1]
    width = heads * HD + LANES
    if last:
        shape = (jax.ShapeDtypeStruct((rows // outer * (len(before) + 1), width), BF),) * outer
    else:
        shape = (jax.ShapeDtypeStruct((rows, width), BF),)
    operands = [query, *before, *tables, *[array for side in sides for array in side]]
    return pl.pallas_call(
        functools.partial(attend_kernel, chunk, outer, core, core_stride, heads, kv_heads, span_len, len(before)),
        out_shape=shape,
        in_specs=[vmem] * len(operands),
        out_specs=(vmem,) * len(shape),
        cost_estimate=pl.CostEstimate(
            flops=4 * core * rows * heads * HD * slots,
            bytes_accessed=4 * core * sides[0][3].size + 4 * rows * heads * HD,
            transcendentals=core * rows * heads * slots,
        ),
        compiler_params=pltpu.CompilerParams(vmem_limit_bytes=10 << 20),
        name="attend",
    )(*operands)


def merge_kernel(groups, count, heads, last, *refs):
    outputs = refs[groups * count :]
    width = heads * HD
    sets = [refs[member * count : (member + 1) * count] for member in range(groups)]
    share = outputs[0].shape[0] // groups

    def store(member, lanes, values):
        for index, out in enumerate(outputs):
            out[member * share : (member + 1) * share, lanes] = values[index * share : (index + 1) * share].astype(BF)

    scaled = []
    for member, parts in enumerate(sets):
        pairs = []
        for part in parts:
            stats = part[:, width:].astype(F32)
            pairs.append(stats + pltpu.roll(stats, LANES - heads, 1))
        top = functools.reduce(jnp.maximum, pairs)
        factors = [jnp.exp2(own - top) for own in pairs]
        total = functools.reduce(
            jnp.add, [f * pltpu.roll(pair, LANES - 2 * heads, 1) for f, pair in zip(factors, pairs)]
        )
        if last:
            inverse = 1.0 / total
            factors = [f * inverse for f in factors]
        else:
            lane = lax.broadcasted_iota(jnp.int32, top.shape, 1)
            packed = jnp.zeros_like(top)
            for place, values in enumerate((*split_pair(top), *split_pair(total))):
                moved = pltpu.roll(values, place * heads, 1) if place else values
                packed = jnp.where(lane // heads == place, moved, packed)
            store(member, slice(width, width + LANES), packed)
        scaled.append(factors)
    for h in range(heads):
        lanes = slice(h * HD, (h + 1) * HD)
        for member, parts in enumerate(sets):
            terms = [f[:, h : h + 1] * part[:, lanes].astype(F32) for f, part in zip(scaled[member], parts)]
            store(member, lanes, functools.reduce(jnp.add, terms))


def merge(groups, pieces, heads, last=False):
    rows = groups[0][0].shape[0]
    count = len(groups[0])
    width = heads * HD + (0 if last else LANES)
    shape = jax.ShapeDtypeStruct((len(groups) * rows // pieces, width), BF)
    vmem = pl.BlockSpec(memory_space=pltpu.VMEM)
    total = len(groups) * count
    return pl.pallas_call(
        functools.partial(merge_kernel, len(groups), count, heads, last),
        out_shape=(shape,) * pieces,
        in_specs=[vmem] * total,
        out_specs=(vmem,) * pieces,
        cost_estimate=pl.CostEstimate(
            flops=4 * total * rows * heads * HD,
            bytes_accessed=2 * (total + len(groups)) * rows * width,
            transcendentals=total * rows * LANES,
        ),
        compiler_params=pltpu.CompilerParams(vmem_limit_bytes=4 << 20),
        name="merge",
    )(*[part for group in groups for part in group])


def per_device(query_in, key_in, value_in, cache_keys, cache_values, live_slots, span_starts):
    devices = lax.axis_size("kv")
    share = query_in.shape[0]
    span_count = span_starts.shape[0]
    span_len = share * devices // span_count
    heads = query_in.shape[1] // HD
    kv_heads = key_in.shape[1] // HD
    stages = stages_of(devices)
    (outer_stride, outer), (inner_stride, inner), (core_stride, core) = stages

    arrived = {k: swap(query_in, k * outer_stride) for k in range(1, outer)}
    other_keys = swap(cache_keys, core_stride)
    other_values = swap(cache_values, core_stride)
    query_own, *tables, limits = prepare(span_len, stages, live_slots.reshape(span_count), span_starts, query_in)
    rows = jnp.concatenate([query_own] + [arrived[k] for k in range(1, outer)], axis=0)
    chunks = [rows] + [swap(rows, i * inner_stride) for i in range(1, inner)]
    sides = [(limits, key_in, value_in, cache_keys, cache_values)]
    small = [swap(array, core_stride) for array in (key_in, value_in, limits)]
    sides.append((small[2], small[0], small[1], other_keys, other_values))
    before = []
    for i, chunk in enumerate(chunks):
        last = i == inner - 1
        parts = attend(i, stages, heads, kv_heads, span_len, chunk, before if last else [], tables, sides, last)
        before += parts if not last else []
    received = [swap(parts[k], k * outer_stride) for k in range(1, outer)]
    kept = merge([[parts[0]] + received], inner, heads)
    received = [swap(kept[k], k * inner_stride) for k in range(1, inner)]
    (attended,) = merge([[kept[0]] + received], 1, heads, last=True)
    return attended


def solution(mesh):
    in_specs = (
        P(("groups", "kv"), None),
        P(("groups", "kv"), None),
        P(("groups", "kv"), None),
        P("groups", "kv", None),
        P("groups", "kv", None),
        P("groups", "kv"),
        P("groups"),
    )
    out_specs = P(("groups", "kv"), None)
    return jax.shard_map(per_device, mesh=mesh, in_specs=in_specs, out_specs=out_specs, check_vma=False)
```

```python
import functools

import jax
import jax.numpy as jnp
import numpy as np
from jax import lax
from jax.experimental import pallas as pl
from jax.experimental.pallas import tpu as pltpu
from jax.sharding import PartitionSpec as P


HD = 128
LANES = 128
NEG_FILL = -1e30
MAX_FLOOR = -5e29
LOG2E = 1.4426950408889634
PREPARE_FLOPS = 10_000_000_000
BF = jnp.bfloat16
F32 = jnp.float32


def turn_table(head_size):
    half_size = head_size // 2
    frequency = 500000.0 ** (-np.arange(half_size) * 2.0 / head_size)
    turn_counts = np.floor(frequency / (2.0 * np.pi) * 2.0**32 + 0.5).astype(np.int64) % 2**32
    turn_counts = np.where(turn_counts >= 2**31, turn_counts - 2**32, turn_counts)
    return turn_counts.astype(np.int32)


def stages_of(devices):
    core = 2 if devices % 2 == 0 else 1
    rest = devices // core
    inner = 1 << ((rest.bit_length() - 1) // 2)
    outer = rest // inner
    return (core * inner, outer), (core, inner), (1, core)


def swap(values, distance):
    devices = lax.axis_size("kv")
    return lax.ppermute(values, "kv", [(i, i ^ distance) for i in range(devices)])


def rotate(values, cosine, signed_sine):
    return values * cosine + pltpu.roll(values, HD // 2, 1) * signed_sine


def split_pair(values):
    high = values.astype(BF).astype(F32)
    return high, (values - high).astype(BF).astype(F32)


def split_index(values, size):
    if size & (size - 1) == 0:
        return values >> (size.bit_length() - 1), values & (size - 1)
    quotient = lax.div(values, jnp.int32(size))
    return quotient, values - quotient * size


def prepare_kernel(share, span_len, stages, start_ref, query_in, query_out, cos_ref, sin_ref, offset_ref):
    (outer_stride, outer), (inner_stride, inner), (core_stride, _) = stages
    spans = start_ref.shape[0]
    me = lax.axis_index("kv")
    query_out[...] = query_in[...]
    lane = lax.broadcasted_iota(jnp.int32, (1, HD), 1)
    pair = jnp.where(lane < HD // 2, lane, lane - HD // 2)
    turns = jnp.zeros((1, HD), jnp.int32)
    for index, turn in enumerate(turn_table(HD)):
        turns = jnp.where(pair == index, jnp.int32(turn), turns)
    row = lax.broadcasted_iota(jnp.int32, cos_ref.shape, 0)
    member, within = split_index(row, share)
    high, low = split_index(member, inner)
    distance = jnp.where(high < outer, high * outer_stride + low * inner_stride, core_stride)
    token = (me ^ distance) * share + within
    span, step = split_index(token, span_len)
    start = jnp.full(cos_ref.shape, start_ref[0], jnp.int32)
    for index in range(1, spans):
        start = jnp.where(span == index, start_ref[index], start)
    angles = ((start + step) * turns).astype(F32) * (2.0 * np.pi / 2.0**32)
    cos_ref[...] = jnp.cos(angles)
    sine = jnp.sin(angles)
    sin_ref[...] = jnp.where(lane < HD // 2, -sine, sine)
    offset_ref[...] = token - me * share


def prepare(span_len, stages, starts, query_in):
    vmem = pl.BlockSpec(memory_space=pltpu.VMEM)
    smem = pl.BlockSpec(memory_space=pltpu.SMEM)
    share = query_in.shape[0]
    rows = share * (stages[0][1] * stages[1][1] + 1)
    table = jax.ShapeDtypeStruct((rows, HD), F32)
    whole = jax.ShapeDtypeStruct((rows, HD), jnp.int32)
    return pl.pallas_call(
        functools.partial(prepare_kernel, share, span_len, stages),
        out_shape=(jax.ShapeDtypeStruct(query_in.shape, BF), table, table, whole),
        in_specs=[smem, vmem],
        out_specs=(vmem,) * 4,
        cost_estimate=pl.CostEstimate(flops=PREPARE_FLOPS, bytes_accessed=12 * rows * HD, transcendentals=2 * rows * HD),
        compiler_params=pltpu.CompilerParams(vmem_limit_bytes=4 << 20),
        name="prepare",
    )(starts, query_in)


def attend_kernel(chunk, relative, core, core_stride, heads, kv_heads, span_len, *refs):
    (query_ref, cos_ref, sin_ref, offset_ref), refs = refs[:4], refs[4:]
    sides = [refs[side * 5 : side * 5 + 5] for side in range(core)]
    (out_ref,) = refs[5 * core :]
    share, slots = sides[0][1].shape[0], sides[0][3].shape[1]
    group = heads // kv_heads
    scale = HD**-0.5 * LOG2E
    rows = query_ref.shape[0]
    me = lax.axis_index("kv")
    own_span, _ = split_index(me * share, span_len)
    span = own_span ^ relative
    has_own = relative == 0
    key_rows = [slice(0, share), slice(cos_ref.shape[0] - share, cos_ref.shape[0])]
    nt = (((1,), (1,)), ((), ()))
    slot = lax.broadcasted_iota(jnp.int32, (1, slots), 1)
    biases = []
    for side in range(core):
        live = sides[side][0][...]
        here = lax.broadcasted_iota(jnp.int32, live.shape, 1) == span
        limit = jnp.sum(jnp.where(here, live, 0).astype(F32), axis=1, keepdims=True).astype(jnp.int32)
        biases.append(jnp.where(slot < limit, 0.0, NEG_FILL))
    lane = lax.broadcasted_iota(jnp.int32, (rows, LANES), 1)
    table = slice(chunk * rows, (chunk + 1) * rows)
    cos, sin = cos_ref[table, :], sin_ref[table, :]
    if has_own:
        other = ((me ^ core_stride) - me) * share - share
        place = jnp.where(lane < share, lane, lane + other)
        admitted = jnp.logical_and(place <= offset_ref[table, :], lane < core * share)
        own_bias = jnp.concatenate([jnp.where(admitted, 0.0, NEG_FILL)] * group, axis=0)

    def stack_new(blocks):
        filler = jnp.zeros((LANES - core * share, HD), F32)
        return jnp.concatenate([*blocks, filler], axis=0).astype(BF)

    raw = {}
    for g in range(kv_heads):
        stacked = []
        for h in range(g * group, (g + 1) * group):
            stacked.append(rotate(query_ref[:, h * HD : (h + 1) * HD].astype(F32), cos, sin))
        query = jnp.concatenate(stacked, axis=0).astype(BF)
        lanes = slice(g * HD, (g + 1) * HD)
        raw[g] = [
            lax.dot_general(query, sides[side][3][span, :, lanes], nt, preferred_element_type=F32)
            for side in range(core)
        ]
        if has_own:
            keys = stack_new(
                [
                    rotate(sides[side][1][:, lanes].astype(F32), cos_ref[key_rows[side], :], sin_ref[key_rows[side], :])
                    for side in range(core)
                ]
            )
            raw[g].append(lax.dot_general(query, keys, nt, preferred_element_type=F32))

    weights, columns = {}, {}
    for g in range(kv_heads):
        scores = [values * scale + bias for values, bias in zip(raw[g], biases + ([own_bias] if has_own else []))]
        top = functools.reduce(jnp.maximum, [jnp.max(values, axis=1, keepdims=True) for values in scores])
        top_high, top_low = split_pair(jnp.maximum(top, MAX_FLOOR))
        top = top_high + top_low
        found = [jnp.exp2(values - top) for values in scores]
        total = functools.reduce(jnp.add, [jnp.sum(values, axis=1, keepdims=True) for values in found])
        weights[g] = [values.astype(BF) for values in found]
        columns[g] = (top_high, top_low, *split_pair(total))

    for g in range(kv_heads):
        lanes = slice(g * HD, (g + 1) * HD)
        terms = [
            jnp.dot(weights[g][side], sides[side][4][span, :, lanes], preferred_element_type=F32) for side in range(core)
        ]
        if has_own:
            values = stack_new([sides[side][2][:, lanes].astype(F32) for side in range(core)])
            terms.append(jnp.dot(weights[g][core], values, preferred_element_type=F32))
        summed = functools.reduce(jnp.add, terms)
        for index in range(group):
            h = g * group + index
            out_ref[:, h * HD : (h + 1) * HD] = summed[index * rows : (index + 1) * rows].astype(BF)

    stats = jnp.zeros((rows, LANES), F32)
    for g in range(kv_heads):
        for index in range(group):
            own = slice(index * rows, (index + 1) * rows)
            for order, values in enumerate(columns[g]):
                stats = jnp.where(lane == order * heads + g * group + index, values[own], stats)
    out_ref[:, heads * HD :] = stats.astype(BF)


def attend(chunk, relative, stages, heads, kv_heads, span_len, query, tables, sides):
    vmem = pl.BlockSpec(memory_space=pltpu.VMEM)
    _, _, (core_stride, core) = stages
    rows, slots = query.shape[0], sides[0][3].shape[1]
    operands = [query, *tables, *[array for side in sides for array in side]]
    return pl.pallas_call(
        functools.partial(attend_kernel, chunk, relative, core, core_stride, heads, kv_heads, span_len),
        out_shape=jax.ShapeDtypeStruct((rows, heads * HD + LANES), BF),
        in_specs=[vmem] * len(operands),
        out_specs=vmem,
        cost_estimate=pl.CostEstimate(
            flops=4 * core * rows * heads * HD * slots,
            bytes_accessed=2 * core * sides[0][3].size + 4 * rows * heads * HD,
            transcendentals=core * rows * heads * slots,
        ),
        compiler_params=pltpu.CompilerParams(vmem_limit_bytes=8 << 20),
        name="attend",
    )(*operands)


def merge_kernel(groups, count, heads, last, *refs):
    outputs = refs[groups * count :]
    width = heads * HD
    sets = [refs[member * count : (member + 1) * count] for member in range(groups)]
    share = outputs[0].shape[0] // groups

    def store(member, lanes, values):
        for index, out in enumerate(outputs):
            out[member * share : (member + 1) * share, lanes] = values[index * share : (index + 1) * share].astype(BF)

    scaled = []
    for member, parts in enumerate(sets):
        pairs = []
        for part in parts:
            stats = part[:, width:].astype(F32)
            pairs.append(stats + pltpu.roll(stats, LANES - heads, 1))
        top = functools.reduce(jnp.maximum, pairs)
        factors = [jnp.exp2(own - top) for own in pairs]
        total = functools.reduce(
            jnp.add, [f * pltpu.roll(pair, LANES - 2 * heads, 1) for f, pair in zip(factors, pairs)]
        )
        if last:
            inverse = 1.0 / total
            factors = [f * inverse for f in factors]
        else:
            lane = lax.broadcasted_iota(jnp.int32, top.shape, 1)
            packed = jnp.zeros_like(top)
            for place, values in enumerate((*split_pair(top), *split_pair(total))):
                moved = pltpu.roll(values, place * heads, 1) if place else values
                packed = jnp.where(lane // heads == place, moved, packed)
            store(member, slice(width, width + LANES), packed)
        scaled.append(factors)
    for h in range(heads):
        lanes = slice(h * HD, (h + 1) * HD)
        for member, parts in enumerate(sets):
            terms = [f[:, h : h + 1] * part[:, lanes].astype(F32) for f, part in zip(scaled[member], parts)]
            store(member, lanes, functools.reduce(jnp.add, terms))


def merge(groups, pieces, heads, last=False):
    rows = groups[0][0].shape[0]
    count = len(groups[0])
    width = heads * HD + (0 if last else LANES)
    shape = jax.ShapeDtypeStruct((len(groups) * rows // pieces, width), BF)
    vmem = pl.BlockSpec(memory_space=pltpu.VMEM)
    total = len(groups) * count
    return pl.pallas_call(
        functools.partial(merge_kernel, len(groups), count, heads, last),
        out_shape=(shape,) * pieces,
        in_specs=[vmem] * total,
        out_specs=(vmem,) * pieces,
        cost_estimate=pl.CostEstimate(
            flops=4 * total * rows * heads * HD,
            bytes_accessed=2 * (total + len(groups)) * rows * width,
            transcendentals=total * rows * LANES,
        ),
        compiler_params=pltpu.CompilerParams(vmem_limit_bytes=4 << 20),
        name="merge",
    )(*[part for group in groups for part in group])


def per_device(query_in, key_in, value_in, cache_keys, cache_values, live_slots, span_starts):
    devices = lax.axis_size("kv")
    share = query_in.shape[0]
    span_count = span_starts.shape[0]
    span_len = share * devices // span_count
    heads = query_in.shape[1] // HD
    kv_heads = key_in.shape[1] // HD
    stages = stages_of(devices)
    (outer_stride, outer), (inner_stride, inner), (core_stride, core) = stages

    arrived = [swap(query_in, i * inner_stride) for i in range(1, inner)]
    other_keys = swap(cache_keys, core_stride)
    other_values = swap(cache_values, core_stride)
    small = (live_slots.reshape(1, span_count), key_in, value_in)
    other_small = [swap(array, core_stride) for array in small]
    query_own, *tables = prepare(span_len, stages, span_starts, query_in)
    rows = jnp.concatenate([query_own] + arrived, axis=0)
    sides = [(*small, cache_keys, cache_values), (*other_small, other_keys, other_values)]
    parts = []
    for k in range(outer):
        chunk = swap(rows, k * outer_stride) if k else rows
        part = attend(k, k * span_count // outer, stages, heads, kv_heads, span_len, chunk, tables, sides)
        parts.append(swap(part, k * outer_stride) if k else part)
    kept = merge([parts], inner, heads)
    received = [swap(kept[i], i * inner_stride) for i in range(1, inner)]
    (attended,) = merge([[kept[0]] + received], 1, heads, last=True)
    return attended


def solution(mesh):
    in_specs = (
        P(("groups", "kv"), None),
        P(("groups", "kv"), None),
        P(("groups", "kv"), None),
        P("groups", "kv", None),
        P("groups", "kv", None),
        P("groups", "kv"),
        P("groups"),
    )
    out_specs = P(("groups", "kv"), None)
    return jax.shard_map(per_device, mesh=mesh, in_specs=in_specs, out_specs=out_specs, check_vma=False)
```

```python
import functools

import jax
import jax.numpy as jnp
import numpy as np
from jax import lax
from jax.experimental import pallas as pl
from jax.experimental.pallas import tpu as pltpu
from jax.sharding import PartitionSpec as P


HD = 128
LANES = 128
NEG_FILL = -1e30
MAX_FLOOR = -5e29
LOG2E = 1.4426950408889634
PREPARE_FLOPS = 10_000_000_000
BF = jnp.bfloat16
F32 = jnp.float32


def turn_table(head_size):
    half_size = head_size // 2
    frequency = 500000.0 ** (-np.arange(half_size) * 2.0 / head_size)
    turn_counts = np.floor(frequency / (2.0 * np.pi) * 2.0**32 + 0.5).astype(np.int64) % 2**32
    turn_counts = np.where(turn_counts >= 2**31, turn_counts - 2**32, turn_counts)
    return turn_counts.astype(np.int32)


def stages_of(devices):
    core = 2 if devices % 2 == 0 else 1
    rest = devices // core
    inner = 1 << ((rest.bit_length() - 1) // 2)
    outer = rest // inner
    return (core * inner, outer), (core, inner), (1, core)


def swap(values, distance):
    devices = lax.axis_size("kv")
    return lax.ppermute(values, "kv", [(i, i ^ distance) for i in range(devices)])


def rotate(values, cosine, signed_sine):
    return values * cosine + pltpu.roll(values, HD // 2, 1) * signed_sine


def split_pair(values):
    high = values.astype(BF).astype(F32)
    return high, (values - high).astype(BF).astype(F32)


def split_index(values, size):
    if size & (size - 1) == 0:
        return values >> (size.bit_length() - 1), values & (size - 1)
    quotient = lax.div(values, jnp.int32(size))
    return quotient, values - quotient * size


def prepare_kernel(share, span_len, stages, start_ref, query_in, query_out, cos_ref, sin_ref, offset_ref):
    (outer_stride, outer), (inner_stride, inner), (core_stride, _) = stages
    spans = start_ref.shape[0]
    me = lax.axis_index("kv")
    query_out[...] = query_in[...]
    lane = lax.broadcasted_iota(jnp.int32, (1, HD), 1)
    pair = jnp.where(lane < HD // 2, lane, lane - HD // 2)
    turns = jnp.zeros((1, HD), jnp.int32)
    for index, turn in enumerate(turn_table(HD)):
        turns = jnp.where(pair == index, jnp.int32(turn), turns)
    row = lax.broadcasted_iota(jnp.int32, cos_ref.shape, 0)
    member, within = split_index(row, share)
    high, low = split_index(member, inner)
    distance = jnp.where(high < outer, high * outer_stride + low * inner_stride, core_stride)
    token = (me ^ distance) * share + within
    span, step = split_index(token, span_len)
    start = jnp.full(cos_ref.shape, start_ref[0], jnp.int32)
    for index in range(1, spans):
        start = jnp.where(span == index, start_ref[index], start)
    angles = ((start + step) * turns).astype(F32) * (2.0 * np.pi / 2.0**32)
    cos_ref[...] = jnp.cos(angles)
    sine = jnp.sin(angles)
    sin_ref[...] = jnp.where(lane < HD // 2, -sine, sine)
    offset_ref[...] = token - me * share


def prepare(span_len, stages, starts, query_in):
    vmem = pl.BlockSpec(memory_space=pltpu.VMEM)
    smem = pl.BlockSpec(memory_space=pltpu.SMEM)
    share = query_in.shape[0]
    rows = share * (stages[0][1] * stages[1][1] + 1)
    table = jax.ShapeDtypeStruct((rows, HD), F32)
    whole = jax.ShapeDtypeStruct((rows, HD), jnp.int32)
    return pl.pallas_call(
        functools.partial(prepare_kernel, share, span_len, stages),
        out_shape=(jax.ShapeDtypeStruct(query_in.shape, BF), table, table, whole),
        in_specs=[smem, vmem],
        out_specs=(vmem,) * 4,
        cost_estimate=pl.CostEstimate(flops=PREPARE_FLOPS, bytes_accessed=12 * rows * HD, transcendentals=2 * rows * HD),
        compiler_params=pltpu.CompilerParams(vmem_limit_bytes=4 << 20),
        name="prepare",
    )(starts, query_in)


def attend_kernel(chunk, relative, core, core_stride, heads, kv_heads, span_len, *refs):
    (query_ref, cos_ref, sin_ref, offset_ref), refs = refs[:4], refs[4:]
    sides = [refs[side * 5 : side * 5 + 5] for side in range(core)]
    outputs = refs[5 * core :]
    piece = outputs[0].shape[0]
    share, slots = sides[0][1].shape[0], sides[0][3].shape[1]
    group = heads // kv_heads
    scale = HD**-0.5 * LOG2E
    rows = query_ref.shape[0]
    me = lax.axis_index("kv")
    own_span, _ = split_index(me * share, span_len)
    span = own_span ^ relative
    has_own = relative == 0
    key_rows = [slice(0, share), slice(cos_ref.shape[0] - share, cos_ref.shape[0])]
    nt = (((1,), (1,)), ((), ()))
    slot = lax.broadcasted_iota(jnp.int32, (1, slots), 1)
    biases = []
    for side in range(core):
        live = sides[side][0][...]
        here = lax.broadcasted_iota(jnp.int32, live.shape, 1) == span
        limit = jnp.sum(jnp.where(here, live, 0).astype(F32), axis=1, keepdims=True).astype(jnp.int32)
        biases.append(jnp.where(slot < limit, 0.0, NEG_FILL))
    lane = lax.broadcasted_iota(jnp.int32, (rows, LANES), 1)
    table = slice(chunk * rows, (chunk + 1) * rows)
    cos, sin = cos_ref[table, :], sin_ref[table, :]
    if has_own:
        other = ((me ^ core_stride) - me) * share - share
        place = jnp.where(lane < share, lane, lane + other)
        admitted = jnp.logical_and(place <= offset_ref[table, :], lane < core * share)
        own_bias = jnp.concatenate([jnp.where(admitted, 0.0, NEG_FILL)] * group, axis=0)

    def stack_new(blocks):
        filler = jnp.zeros((LANES - core * share, HD), F32)
        return jnp.concatenate([*blocks, filler], axis=0).astype(BF)

    raw = {}
    for g in range(kv_heads):
        stacked = []
        for h in range(g * group, (g + 1) * group):
            stacked.append(rotate(query_ref[:, h * HD : (h + 1) * HD].astype(F32), cos, sin))
        query = jnp.concatenate(stacked, axis=0).astype(BF)
        lanes = slice(g * HD, (g + 1) * HD)
        raw[g] = [
            lax.dot_general(query, sides[side][3][span, :, lanes], nt, preferred_element_type=F32)
            for side in range(core)
        ]
        if has_own:
            keys = stack_new(
                [
                    rotate(sides[side][1][:, lanes].astype(F32), cos_ref[key_rows[side], :], sin_ref[key_rows[side], :])
                    for side in range(core)
                ]
            )
            raw[g].append(lax.dot_general(query, keys, nt, preferred_element_type=F32))

    weights, columns = {}, {}
    for g in range(kv_heads):
        scores = [values * scale + bias for values, bias in zip(raw[g], biases + ([own_bias] if has_own else []))]
        top = functools.reduce(jnp.maximum, [jnp.max(values, axis=1, keepdims=True) for values in scores])
        top_high, top_low = split_pair(jnp.maximum(top, MAX_FLOOR))
        top = top_high + top_low
        found = [jnp.exp2(values - top) for values in scores]
        total = functools.reduce(jnp.add, [jnp.sum(values, axis=1, keepdims=True) for values in found])
        weights[g] = [values.astype(BF) for values in found]
        columns[g] = (top_high, top_low, *split_pair(total))

    for g in range(kv_heads):
        lanes = slice(g * HD, (g + 1) * HD)
        terms = [
            jnp.dot(weights[g][side], sides[side][4][span, :, lanes], preferred_element_type=F32) for side in range(core)
        ]
        if has_own:
            values = stack_new([sides[side][2][:, lanes].astype(F32) for side in range(core)])
            terms.append(jnp.dot(weights[g][core], values, preferred_element_type=F32))
        summed = functools.reduce(jnp.add, terms)
        for index in range(group):
            h = g * group + index
            for n, out in enumerate(outputs):
                at = index * rows + n * piece
                out[:, h * HD : (h + 1) * HD] = summed[at : at + piece].astype(BF)

    head, place = lane % heads, lane // heads
    stats = []
    for g in range(kv_heads):
        found = jnp.zeros((rows, LANES), F32)
        for index in range(group):
            own = slice(index * rows, (index + 1) * rows)
            first, second, third, fourth = (values[own] for values in columns[g])
            values = jnp.where(place < 2, jnp.where(place == 0, first, second), jnp.where(place == 2, third, fourth))
            found = jnp.where(head == g * group + index, values, found)
        stats.append(found)
    packed = functools.reduce(jnp.add, stats)
    for n, out in enumerate(outputs):
        out[:, heads * HD :] = packed[n * piece : (n + 1) * piece].astype(BF)


def attend(chunk, relative, stages, heads, kv_heads, span_len, query, tables, sides):
    vmem = pl.BlockSpec(memory_space=pltpu.VMEM)
    _, _, (core_stride, core) = stages
    rows, slots = query.shape[0], sides[0][3].shape[1]
    operands = [query, *tables, *[array for side in sides for array in side]]
    return pl.pallas_call(
        functools.partial(attend_kernel, chunk, relative, core, core_stride, heads, kv_heads, span_len),
        out_shape=(jax.ShapeDtypeStruct((rows // stages[1][1], heads * HD + LANES), BF),) * stages[1][1],
        in_specs=[vmem] * len(operands),
        out_specs=(vmem,) * stages[1][1],
        cost_estimate=pl.CostEstimate(
            flops=4 * core * rows * heads * HD * slots,
            bytes_accessed=2 * core * sides[0][3].size + 4 * rows * heads * HD,
            transcendentals=core * rows * heads * slots,
        ),
        compiler_params=pltpu.CompilerParams(vmem_limit_bytes=8 << 20),
        name="attend",
    )(*operands)


def merge_kernel(groups, count, heads, last, *refs):
    outputs = refs[groups * count :]
    width = heads * HD
    sets = [refs[member * count : (member + 1) * count] for member in range(groups)]
    share = outputs[0].shape[0] // groups

    def store(member, lanes, values):
        for index, out in enumerate(outputs):
            out[member * share : (member + 1) * share, lanes] = values[index * share : (index + 1) * share].astype(BF)

    scaled = []
    for member, parts in enumerate(sets):
        pairs = []
        for part in parts:
            stats = part[:, width:].astype(F32)
            pairs.append(stats + pltpu.roll(stats, LANES - heads, 1))
        top = functools.reduce(jnp.maximum, pairs)
        factors = [jnp.exp2(own - top) for own in pairs]
        total = functools.reduce(
            jnp.add, [f * pltpu.roll(pair, LANES - 2 * heads, 1) for f, pair in zip(factors, pairs)]
        )
        if last:
            inverse = 1.0 / total
            factors = [f * inverse for f in factors]
        else:
            lane = lax.broadcasted_iota(jnp.int32, top.shape, 1)
            packed = jnp.zeros_like(top)
            for place, values in enumerate((*split_pair(top), *split_pair(total))):
                moved = pltpu.roll(values, place * heads, 1) if place else values
                packed = jnp.where(lane // heads == place, moved, packed)
            store(member, slice(width, width + LANES), packed)
        scaled.append(factors)
    for h in range(heads):
        lanes = slice(h * HD, (h + 1) * HD)
        for member, parts in enumerate(sets):
            terms = [f[:, h : h + 1] * part[:, lanes].astype(F32) for f, part in zip(scaled[member], parts)]
            store(member, lanes, functools.reduce(jnp.add, terms))


def merge(groups, pieces, heads, last=False):
    rows = groups[0][0].shape[0]
    count = len(groups[0])
    width = heads * HD + (0 if last else LANES)
    shape = jax.ShapeDtypeStruct((len(groups) * rows // pieces, width), BF)
    vmem = pl.BlockSpec(memory_space=pltpu.VMEM)
    total = len(groups) * count
    return pl.pallas_call(
        functools.partial(merge_kernel, len(groups), count, heads, last),
        out_shape=(shape,) * pieces,
        in_specs=[vmem] * total,
        out_specs=(vmem,) * pieces,
        cost_estimate=pl.CostEstimate(
            flops=4 * total * rows * heads * HD,
            bytes_accessed=2 * (total + len(groups)) * rows * width,
            transcendentals=total * rows * LANES,
        ),
        compiler_params=pltpu.CompilerParams(vmem_limit_bytes=4 << 20),
        name="merge",
    )(*[part for group in groups for part in group])


def per_device(query_in, key_in, value_in, cache_keys, cache_values, live_slots, span_starts):
    devices = lax.axis_size("kv")
    share = query_in.shape[0]
    span_count = span_starts.shape[0]
    span_len = share * devices // span_count
    heads = query_in.shape[1] // HD
    kv_heads = key_in.shape[1] // HD
    stages = stages_of(devices)
    (outer_stride, outer), (inner_stride, inner), (core_stride, core) = stages

    arrived = [swap(query_in, i * inner_stride) for i in range(1, inner)]
    other_keys = swap(cache_keys, core_stride)
    other_values = swap(cache_values, core_stride)
    small = (live_slots.reshape(1, span_count), key_in, value_in)
    other_small = [swap(array, core_stride) for array in small]
    query_own, *tables = prepare(span_len, stages, span_starts, query_in)
    rows = jnp.concatenate([query_own] + arrived, axis=0)
    sides = [(*small, cache_keys, cache_values), (*other_small, other_keys, other_values)]
    parts = []
    for k in range(outer):
        chunk = swap(rows, k * outer_stride) if k else rows
        pieces = attend(k, k * span_count // outer, stages, heads, kv_heads, span_len, chunk, tables, sides)
        for i, piece in enumerate(pieces):
            distance = k * outer_stride + i * inner_stride
            parts.append(swap(piece, distance) if distance else piece)
    (attended,) = merge([parts], 1, heads, last=True)
    return attended


def solution(mesh):
    in_specs = (
        P(("groups", "kv"), None),
        P(("groups", "kv"), None),
        P(("groups", "kv"), None),
        P("groups", "kv", None),
        P("groups", "kv", None),
        P("groups", "kv"),
        P("groups"),
    )
    out_specs = P(("groups", "kv"), None)
    return jax.shard_map(per_device, mesh=mesh, in_specs=in_specs, out_specs=out_specs, check_vma=False)
```

```python
import functools

import jax
import jax.numpy as jnp
import numpy as np
from jax import lax
from jax.experimental import pallas as pl
from jax.experimental.pallas import tpu as pltpu
from jax.sharding import PartitionSpec as P


HD = 128
LANES = 128
NEG_FILL = -1e30
MAX_FLOOR = -5e29
LOG2E = 1.4426950408889634
PREPARE_FLOPS = 10_000_000_000
BF = jnp.bfloat16
F32 = jnp.float32


def turn_table(head_size):
    half_size = head_size // 2
    frequency = 500000.0 ** (-np.arange(half_size) * 2.0 / head_size)
    turn_counts = np.floor(frequency / (2.0 * np.pi) * 2.0**32 + 0.5).astype(np.int64) % 2**32
    turn_counts = np.where(turn_counts >= 2**31, turn_counts - 2**32, turn_counts)
    return turn_counts.astype(np.int32)


def stages_of(devices):
    core = 2 if devices % 2 == 0 else 1
    rest = devices // core
    inner = 1 << ((rest.bit_length() - 1) // 2)
    outer = rest // inner
    return (core * inner, outer), (core, inner), (1, core)


def shares_of(devices):
    (outer_stride, outer), (inner_stride, inner), _ = stages_of(devices)
    shares = []
    for o in range(outer):
        for i in range(0, inner, 2):
            pair = [o * outer_stride + i * inner_stride, o * outer_stride + (i + 1) * inner_stride]
            shares.append(tuple(pair[::-1] if o % 2 else pair))
    return shares


def swap(values, distance, odd_distance=None):
    devices = lax.axis_size("kv")
    odd_distance = distance if odd_distance is None else odd_distance
    by_core = (distance, odd_distance)
    return lax.ppermute(values, "kv", [(i, i ^ by_core[i % 2]) for i in range(devices) if by_core[i % 2]])


def rotate(values, cosine, signed_sine):
    return values * cosine + pltpu.roll(values, HD // 2, 1) * signed_sine


def split_pair(values):
    high = values.astype(BF).astype(F32)
    return high, (values - high).astype(BF).astype(F32)


def split_index(values, size):
    if size & (size - 1) == 0:
        return values >> (size.bit_length() - 1), values & (size - 1)
    quotient = lax.div(values, jnp.int32(size))
    return quotient, values - quotient * size


def prepare_kernel(share, span_len, shares, start_ref, query_in, query_out, cos_ref, sin_ref, offset_ref):
    spans = start_ref.shape[0]
    me = lax.axis_index("kv")
    query_out[...] = query_in[...]
    lane = lax.broadcasted_iota(jnp.int32, (1, HD), 1)
    pair = jnp.where(lane < HD // 2, lane, lane - HD // 2)
    turns = jnp.zeros((1, HD), jnp.int32)
    for index, turn in enumerate(turn_table(HD)):
        turns = jnp.where(pair == index, jnp.int32(turn), turns)
    row = lax.broadcasted_iota(jnp.int32, cos_ref.shape, 0)
    member, within = split_index(row, share)
    block, side = member >> 1, member & 1
    distance = side
    for n, (even, odd) in enumerate(shares):
        distance = jnp.where(block == n, side + jnp.where((me & 1) == 0, even, odd), distance)
    token = (me ^ distance) * share + within
    span, step = split_index(token, span_len)
    start = jnp.full(cos_ref.shape, start_ref[0], jnp.int32)
    for index in range(1, spans):
        start = jnp.where(span == index, start_ref[index], start)
    angles = ((start + step) * turns).astype(F32) * (2.0 * np.pi / 2.0**32)
    cos_ref[...] = jnp.cos(angles)
    sine = jnp.sin(angles)
    sin_ref[...] = jnp.where(lane < HD // 2, -sine, sine)
    offset_ref[...] = token - me * share


def prepare(span_len, shares, starts, query_in):
    vmem = pl.BlockSpec(memory_space=pltpu.VMEM)
    smem = pl.BlockSpec(memory_space=pltpu.SMEM)
    share = query_in.shape[0]
    rows = 2 * share * (len(shares) + 1)
    table = jax.ShapeDtypeStruct((rows, HD), F32)
    whole = jax.ShapeDtypeStruct((rows, HD), jnp.int32)
    return pl.pallas_call(
        functools.partial(prepare_kernel, share, span_len, shares),
        out_shape=(jax.ShapeDtypeStruct(query_in.shape, BF), table, table, whole),
        in_specs=[smem, vmem],
        out_specs=(vmem,) * 4,
        cost_estimate=pl.CostEstimate(flops=PREPARE_FLOPS, bytes_accessed=12 * rows * HD, transcendentals=2 * rows * HD),
        compiler_params=pltpu.CompilerParams(vmem_limit_bytes=4 << 20),
        name="prepare",
    )(starts, query_in)


def attend_kernel(chunk, distances, heads, kv_heads, span_len, *refs):
    core, core_stride, has_own = 2, 1, True
    (query_ref, cos_ref, sin_ref, offset_ref), refs = refs[:4], refs[4:]
    sides = [refs[side * 5 : side * 5 + 5] for side in range(core)]
    (out_ref,) = refs[5 * core :]
    share, slots = sides[0][1].shape[0], sides[0][3].shape[1]
    group = heads // kv_heads
    scale = HD**-0.5 * LOG2E
    rows = query_ref.shape[0]
    me = lax.axis_index("kv")
    own_span, _ = split_index(me * share, span_len)
    span, _ = split_index((me ^ jnp.where((me & 1) == 0, distances[0], distances[1])) * share, span_len)
    last = cos_ref.shape[0]
    key_rows = [slice(last - 2 * share, last - share), slice(last - share, last)]
    nt = (((1,), (1,)), ((), ()))
    slot = lax.broadcasted_iota(jnp.int32, (1, slots), 1)
    biases = []
    for side in range(core):
        live = sides[side][0][...]
        here = lax.broadcasted_iota(jnp.int32, live.shape, 1) == span
        limit = jnp.sum(jnp.where(here, live, 0).astype(F32), axis=1, keepdims=True).astype(jnp.int32)
        biases.append(jnp.where(slot < limit, 0.0, NEG_FILL))
    lane = lax.broadcasted_iota(jnp.int32, (rows, LANES), 1)
    table = slice(chunk * rows, (chunk + 1) * rows)
    cos, sin = cos_ref[table, :], sin_ref[table, :]
    if has_own:
        other = ((me ^ core_stride) - me) * share - share
        place = jnp.where(lane < share, lane, lane + other)
        width = jnp.where(span == own_span, core * share, 0)
        admitted = jnp.logical_and(place <= offset_ref[table, :], lane < width)
        own_bias = jnp.concatenate([jnp.where(admitted, 0.0, NEG_FILL)] * group, axis=0)

    def stack_new(blocks):
        filler = jnp.zeros((LANES - core * share, HD), F32)
        return jnp.concatenate([*blocks, filler], axis=0).astype(BF)

    raw = {}
    for g in range(kv_heads):
        stacked = []
        for h in range(g * group, (g + 1) * group):
            stacked.append(rotate(query_ref[:, h * HD : (h + 1) * HD].astype(F32), cos, sin))
        query = jnp.concatenate(stacked, axis=0).astype(BF)
        lanes = slice(g * HD, (g + 1) * HD)
        raw[g] = [
            lax.dot_general(query, sides[side][3][span, :, lanes], nt, preferred_element_type=F32)
            for side in range(core)
        ]
        if has_own:
            keys = stack_new(
                [
                    rotate(sides[side][1][:, lanes].astype(F32), cos_ref[key_rows[side], :], sin_ref[key_rows[side], :])
                    for side in range(core)
                ]
            )
            raw[g].append(lax.dot_general(query, keys, nt, preferred_element_type=F32))

    weights, columns = {}, {}
    for g in range(kv_heads):
        scores = [values * scale + bias for values, bias in zip(raw[g], biases + ([own_bias] if has_own else []))]
        top = functools.reduce(jnp.maximum, [jnp.max(values, axis=1, keepdims=True) for values in scores])
        top_high, top_low = split_pair(jnp.maximum(top, MAX_FLOOR))
        top = top_high + top_low
        found = [jnp.exp2(values - top) for values in scores]
        total = functools.reduce(jnp.add, [jnp.sum(values, axis=1, keepdims=True) for values in found])
        weights[g] = [values.astype(BF) for values in found]
        columns[g] = (top_high, top_low, *split_pair(total))

    for g in range(kv_heads):
        lanes = slice(g * HD, (g + 1) * HD)
        terms = [
            jnp.dot(weights[g][side], sides[side][4][span, :, lanes], preferred_element_type=F32) for side in range(core)
        ]
        if has_own:
            values = stack_new([sides[side][2][:, lanes].astype(F32) for side in range(core)])
            terms.append(jnp.dot(weights[g][core], values, preferred_element_type=F32))
        summed = functools.reduce(jnp.add, terms)
        for index in range(group):
            h = g * group + index
            out_ref[:, h * HD : (h + 1) * HD] = summed[index * rows : (index + 1) * rows].astype(BF)

    head, place = lane % heads, lane // heads
    stats = []
    for g in range(kv_heads):
        found = jnp.zeros((rows, LANES), F32)
        for index in range(group):
            own = slice(index * rows, (index + 1) * rows)
            first, second, third, fourth = (values[own] for values in columns[g])
            values = jnp.where(place < 2, jnp.where(place == 0, first, second), jnp.where(place == 2, third, fourth))
            found = jnp.where(head == g * group + index, values, found)
        stats.append(found)
    out_ref[:, heads * HD :] = functools.reduce(jnp.add, stats).astype(BF)


def attend(chunk, distances, heads, kv_heads, span_len, query, tables, sides):
    vmem = pl.BlockSpec(memory_space=pltpu.VMEM)
    core = len(sides)
    rows, slots = query.shape[0], sides[0][3].shape[1]
    operands = [query, *tables, *[array for side in sides for array in side]]
    return pl.pallas_call(
        functools.partial(attend_kernel, chunk, distances, heads, kv_heads, span_len),
        out_shape=jax.ShapeDtypeStruct((rows, heads * HD + LANES), BF),
        in_specs=[vmem] * len(operands),
        out_specs=vmem,
        cost_estimate=pl.CostEstimate(
            flops=4 * core * rows * heads * HD * slots,
            bytes_accessed=2 * core * sides[0][3].size + 4 * rows * heads * HD,
            transcendentals=core * rows * heads * slots,
        ),
        compiler_params=pltpu.CompilerParams(vmem_limit_bytes=8 << 20),
        name="attend",
    )(*operands)


def merge_kernel(groups, count, heads, last, *refs):
    outputs = refs[groups * count :]
    width = heads * HD
    sets = [refs[member * count : (member + 1) * count] for member in range(groups)]
    share = outputs[0].shape[0] // groups

    def store(member, lanes, values):
        for index, out in enumerate(outputs):
            out[member * share : (member + 1) * share, lanes] = values[index * share : (index + 1) * share].astype(BF)

    scaled = []
    for member, parts in enumerate(sets):
        pairs = []
        for part in parts:
            stats = part[:, width:].astype(F32)
            pairs.append(stats + pltpu.roll(stats, LANES - heads, 1))
        top = functools.reduce(jnp.maximum, pairs)
        factors = [jnp.exp2(own - top) for own in pairs]
        total = functools.reduce(
            jnp.add, [f * pltpu.roll(pair, LANES - 2 * heads, 1) for f, pair in zip(factors, pairs)]
        )
        if last:
            inverse = 1.0 / total
            factors = [f * inverse for f in factors]
        else:
            lane = lax.broadcasted_iota(jnp.int32, top.shape, 1)
            packed = jnp.zeros_like(top)
            for place, values in enumerate((*split_pair(top), *split_pair(total))):
                moved = pltpu.roll(values, place * heads, 1) if place else values
                packed = jnp.where(lane // heads == place, moved, packed)
            store(member, slice(width, width + LANES), packed)
        scaled.append(factors)
    for h in range(heads):
        lanes = slice(h * HD, (h + 1) * HD)
        for member, parts in enumerate(sets):
            terms = [f[:, h : h + 1] * part[:, lanes].astype(F32) for f, part in zip(scaled[member], parts)]
            store(member, lanes, functools.reduce(jnp.add, terms))


def merge(groups, pieces, heads, last=False):
    rows = groups[0][0].shape[0]
    count = len(groups[0])
    width = heads * HD + (0 if last else LANES)
    shape = jax.ShapeDtypeStruct((len(groups) * rows // pieces, width), BF)
    vmem = pl.BlockSpec(memory_space=pltpu.VMEM)
    total = len(groups) * count
    return pl.pallas_call(
        functools.partial(merge_kernel, len(groups), count, heads, last),
        out_shape=(shape,) * pieces,
        in_specs=[vmem] * total,
        out_specs=(vmem,) * pieces,
        cost_estimate=pl.CostEstimate(
            flops=4 * total * rows * heads * HD,
            bytes_accessed=2 * (total + len(groups)) * rows * width,
            transcendentals=total * rows * LANES,
        ),
        compiler_params=pltpu.CompilerParams(vmem_limit_bytes=4 << 20),
        name="merge",
    )(*[part for group in groups for part in group])


def per_device(query_in, key_in, value_in, cache_keys, cache_values, live_slots, span_starts):
    devices = lax.axis_size("kv")
    me = lax.axis_index("kv")
    share = query_in.shape[0]
    span_count = span_starts.shape[0]
    span_len = share * devices // span_count
    heads = query_in.shape[1] // HD
    kv_heads = key_in.shape[1] // HD
    shares = shares_of(devices)
    even_core = me % 2 == 0

    other_query = swap(query_in, 1)
    other_keys = swap(cache_keys, 1)
    other_values = swap(cache_values, 1)
    small = (live_slots.reshape(1, span_count), key_in, value_in)
    other_small = [swap(array, 1) for array in small]
    query_own, *tables = prepare(span_len, shares, span_starts, query_in)
    rows = jnp.concatenate([query_own, other_query], axis=0)
    sides = [(*small, cache_keys, cache_values), (*other_small, other_keys, other_values)]
    parts = []
    for n, (even, odd) in enumerate(shares):
        chunk = swap(rows, even, odd)
        chunk = chunk if even else jnp.where(even_core, rows, chunk)
        part = attend(n, (even, odd), heads, kv_heads, span_len, chunk, tables, sides)
        back = swap(part, even, odd)
        parts.append(back if even else jnp.where(even_core, part, back))
    kept, sent = merge([parts], 2, heads)
    (attended,) = merge([[kept, swap(sent, 1)]], 1, heads, last=True)
    return attended


def solution(mesh):
    in_specs = (
        P(("groups", "kv"), None),
        P(("groups", "kv"), None),
        P(("groups", "kv"), None),
        P("groups", "kv", None),
        P("groups", "kv", None),
        P("groups", "kv"),
        P("groups"),
    )
    out_specs = P(("groups", "kv"), None)
    return jax.shard_map(per_device, mesh=mesh, in_specs=in_specs, out_specs=out_specs, check_vma=False)
```
